512 devices in a mesh: sec: 2 (over x_hi), ax: 16 (over y, core), az: 16 (over x_lo, z).
Axes of the slice: x: 4 (x_hi: 2, x_lo: 2; x = x_hi * 2 + x_lo), y: 8, z: 8, core: 2. Of those that a mesh axis runs over, the one named last changes fastest.
Arguments:
- fields: float32 [2, 4, 256, 256, 256], P('sec', None, 'ax', 'az'), may hold values from -6 to 6
- coefficients: float32 [2, 3, 256, 256, 256], P('sec', None, 'ax', 'az'), may hold values from -0.8 to 0.8, as said below
- old_source: float32 [4, 256, 256, 256], P(None, 'ax', 'az'), may hold values from -6 to 6
- weight_blocks: bfloat16 [16, 16, 8, 128, 128], P('ax', 'az'), may hold values from -0.5 to 0.5
- send_ids: int32 [16, 16, 16, 8], P('ax', 'az'), may hold values from -1 to 511, as said below
- target_ids: int32 [16, 16, 16, 8], P('ax', 'az'), may hold values from 0 to 511
- weight_ids: int32 [16, 16, 16, 8], P('ax', 'az'), may hold values from 0 to 7
Outputs:
- advanced: float32 [2, 4, 256, 256, 256], P('sec', None, 'ax', 'az')
The draws below stay inside these ranges and needn't reach their ends.
Inputs may be any that keep to these rules, and one draw needn't show every extreme that they name: `send_ids`: entries are -1 (an empty slot) or a block index of the sending device; empty slots follow the live ones in a list. In each sector one cycle, drawn from the seed, receives full lists of 8 live slots from every device of that sector; lists to the other cycles hold fewer than 8 live slots, at most a number that shrinks the farther the cycle lies from that one. A block index appears at most once among one device's lists. `coefficients`: section 0 holds positive viscosities, section 1 the mean flow.
All inputs are finite; a program needn't handle non-finite values.
Results may differ from the reference program's by a relative error of at most 0.0004.
Values may be sent and summed in bfloat16 or wider, within the bound.
No kernel may reach another device: no remote copies, remote signals or barrier semaphores. Data moves between devices by JAX's collectives and lax.ppermute only.
A program may use at most 64 MiB of HBM per device.

```python
import jax
import jax.numpy as jnp
from jax import lax

C1 = 16
C2 = 16
C3 = 256
NV = 4
LINE = 128
CAP = 8
NW = 8
N1 = 256
N2 = 256
NB = 512
N_AX = 16
N_AZ = 16


def draw_coefficients(key, part):
    first_key, second_key = jax.random.split(key)
    shape = (3, N1, N2, C3)
    spread = jax.random.uniform(first_key, shape, jnp.float32)
    flow_draw = jax.random.uniform(second_key, shape, jnp.float32, -1.0, 1.0)
    viscosity = 0.1 * jnp.exp(jnp.log(6.0) * spread)
    flow = jnp.stack([0.3 * flow_draw[0], 0.3 * flow_draw[1], 0.4 + 0.4 * flow_draw[2]])
    return jnp.stack([viscosity, flow]).astype(jnp.float32)


def draw_send_ids(key, part):
    cycle_count = N1 // C1
    sector_count = N2 // C2
    count_key, order_key, cycle_key = jax.random.split(jax.random.fold_in(key, 17), 3)
    order_keys = jax.random.split(order_key, cycle_count * sector_count)
    orders = jax.vmap(lambda member: jax.random.permutation(member, NB))(order_keys)
    chosen = orders[:, :cycle_count * CAP].reshape(cycle_count, sector_count, cycle_count, CAP).astype(jnp.int32)
    cycles = jnp.arange(cycle_count, dtype=jnp.int32)
    full_cycle = jax.random.randint(cycle_key, (sector_count,), 0, cycle_count, dtype=jnp.int32)
    distance = jnp.abs(cycles[None, :] - full_cycle[:, None])
    highest = jnp.clip((CAP * (cycle_count - distance) + cycle_count - 1) // cycle_count, 0, CAP - 1)
    raw_counts = jax.random.randint(count_key, (cycle_count, sector_count, cycle_count), 0, 1 << 20, dtype=jnp.int32)
    counts = raw_counts % (highest + 1)[None, :, :]
    counts = jnp.where(distance[None, :, :] == 0, CAP, counts)
    slots = jnp.arange(CAP, dtype=jnp.int32)
    return jnp.where(slots[None, None, None, :] < counts[..., None], chosen, -1).astype(jnp.int32)


def set_ends(values, own_key, least, top_value):
    longest = values.shape.index(max(values.shape))
    spots = []
    for shift in (0, 1):
        where = [jax.random.randint(jax.random.fold_in(own_key, axis), (), 0, length) for axis, length in enumerate(values.shape)]
        where[longest] = (where[longest] + shift) % values.shape[longest]
        spots.append(tuple(where))
    return values.at[spots[0]].set(least).at[spots[1]].set(top_value)


def level_of(stream_key, dims, cuts, least, top_value):
    loudness = 1.0
    for position, blocks in cuts:
        heights = jax.random.uniform(jax.random.fold_in(jax.random.fold_in(stream_key, 6), position), (blocks,), jnp.float32, least / len(cuts), top_value / len(cuts))
        loudness = loudness * jnp.repeat(jnp.exp(heights), dims[position] // blocks).reshape((-1,) + (1,) * (len(dims) - 1 - position))
    return loudness


def noise(key, extent, width, most, shards=(), held_as=jnp.bfloat16):
    values = jax.random.normal(key, extent, jnp.float32) * width
    if len(shards) > 0:
        values = level_of(key, extent, shards, -0.22, 0.18) * values
    return jnp.clip(values, min=-most, max=most).astype(held_as)


def setup_inputs(seed: int = 0) -> dict:
    arg_keys = jax.random.split(jax.random.key(seed), 8)
    fields = noise(arg_keys[0], (2, NV, N1, N2, C3), 1.0, 6.0, ((0, 2), (2, 16), (3, 16)), jnp.float32)
    coefficients = draw_coefficients(jax.random.fold_in(arg_keys[7], 71), 0)
    old_source = noise(arg_keys[2], (NV, N1, N2, C3), 1.0, 6.0, ((1, 16), (2, 16)), jnp.float32)
    weight_blocks = noise(arg_keys[3], (N_AX, N_AZ, NW, LINE, LINE), LINE ** -0.5, 0.5, ((0, 16), (1, 16)))
    send_ids = draw_send_ids(jax.random.fold_in(arg_keys[7], 71), 0)
    target_ids = set_ends(jax.random.randint(arg_keys[5], (N_AX, N_AZ, N_AX, CAP), 0, NB), jax.random.fold_in(arg_keys[5], 1), 0, NB - 1).astype(jnp.int32)
    weight_ids = set_ends(jax.random.randint(arg_keys[6], (N_AX, N_AZ, N_AX, CAP), 0, NW), jax.random.fold_in(arg_keys[6], 1), 0, NW - 1).astype(jnp.int32)
    return dict(fields=fields, coefficients=coefficients, old_source=old_source, weight_blocks=weight_blocks, send_ids=send_ids, target_ids=target_ids, weight_ids=weight_ids)


STEP = 0.25


def neighbours(bordered, direction):
    upper_index = [slice(None), slice(1, -1), slice(1, -1), slice(1, -1)]
    lower_index = [slice(None), slice(1, -1), slice(1, -1), slice(1, -1)]
    upper_index[direction] = slice(2, None)
    lower_index[direction] = slice(None, -2)
    return bordered[tuple(upper_index)], bordered[tuple(lower_index)]


def advance(padded, factors, source, acoustic):
    bordered = jnp.pad(padded, ((0, 0), (0, 0), (0, 0), (1, 1)))
    middle = bordered[:, 1:-1, 1:-1, 1:-1]
    tendency = jnp.zeros_like(middle)
    couple_first = jnp.zeros_like(middle[0])
    couple_rest = []
    for direction in range(3):
        upper_cells, lower_cells = neighbours(bordered, direction + 1)
        gradient = 0.5 * (upper_cells - lower_cells)
        if acoustic:
            tendency = tendency - factors[direction] * gradient
            couple_first = couple_first + gradient[direction + 1]
            couple_rest.append(gradient[0])
        else:
            tendency = tendency - middle[direction] * gradient + factors[direction] * (upper_cells - 2.0 * middle + lower_cells)
    if acoustic:
        coupling = jnp.stack([couple_first] + couple_rest)
        tendency = tendency - coupling + source
    return middle + STEP * tendency


def widen(values):
    bordered = jnp.pad(values, ((0, 0), (1, 1), (0, 0), (0, 0)))
    return jnp.concatenate([bordered[:, :, -1:], bordered, bordered[:, :, :1]], axis=2)


def cut_blocks(values):
    shaped = values.reshape(NV, N_AX, C1, N_AZ, C2, C3)
    shaped = shaped.transpose(1, 3, 0, 2, 4, 5)
    return shaped.reshape(N_AX, N_AZ, NV, NB, LINE)


def reference(fields, coefficients, old_source, weight_blocks, send_ids, target_ids, weight_ids):
    les_first = advance(widen(fields[0]), coefficients[0], None, False)
    acoustic_first = advance(widen(fields[1]), coefficients[1], old_source, True)
    line_blocks = cut_blocks(les_first).astype(jnp.bfloat16)
    slot_count = N_AX * CAP

    def one_tile(tile_index):
        cycle = tile_index // N_AZ
        sector = tile_index % N_AZ
        sector_blocks = line_blocks[:, sector]
        wanted = send_ids[:, sector, cycle, :]
        clipped = jnp.maximum(wanted, 0).astype(jnp.int32)
        picked = jax.vmap(lambda source_blocks, block_ids: jnp.take(source_blocks, block_ids, axis=1))(sector_blocks, clipped)
        picked = jnp.where((wanted >= 0)[:, None, :, None], picked, jnp.zeros_like(picked))
        line_data = picked.transpose(1, 0, 2, 3).reshape(NV, slot_count, LINE)
        tile_weights = weight_blocks[cycle, sector]
        chosen = jnp.take(tile_weights, weight_ids[cycle, sector].reshape(slot_count).astype(jnp.int32), axis=0)
        contribution = jnp.einsum("sij,vsj->svi", chosen.astype(jnp.float32), line_data.astype(jnp.float32))
        summed = jax.ops.segment_sum(contribution.reshape(slot_count, NV * LINE), target_ids[cycle, sector].reshape(slot_count).astype(jnp.int32), num_segments=NB)
        return summed.reshape(NB, NV, LINE).transpose(1, 0, 2)

    tiles = lax.map(one_tile, jnp.arange(N_AX * N_AZ, dtype=jnp.int32))
    new_source = tiles.reshape(N_AX, N_AZ, NV, C1, C2, C3).transpose(2, 0, 3, 1, 4, 5).reshape(NV, N1, N2, C3)
    les_second = advance(widen(les_first), coefficients[0], None, False)
    acoustic_second = advance(widen(acoustic_first), coefficients[1], new_source, True)
    return jnp.stack([les_second, acoustic_second])
```

```python
import jax
import jax.numpy as jnp
from jax import lax
from jax.experimental import pallas as pl
from jax.experimental.pallas import tpu as pltpu
from jax.sharding import PartitionSpec as P

F32 = jnp.float32
BF16 = jnp.bfloat16
NV = 4
C1 = 16
C2 = 16
C3 = 256
LINE = 128
CAP = 8
NW = 8

NEAR = 0
FAR = 4
COEF = 8
SOURCE = 11
CORNER = 15
PLANES = 16

VMEM = pl.BlockSpec(memory_space=pltpu.VMEM)
SMEM = pl.BlockSpec(memory_space=pltpu.SMEM)


def shift(x, axis, by, periodic):
    count = lax.axis_size(axis)
    pairs = [(i, (i + by) % count) for i in range(count) if periodic or 0 <= i + by < count]
    return lax.ppermute(x, axis, pairs)


def rows_of(shape, axis):
    return lax.broadcasted_iota(jnp.int32, shape, axis)


def next_row(x, end):
    return jnp.where(rows_of(x.shape, 0) == x.shape[0] - 1, end, pltpu.roll(x, x.shape[0] - 1, 0))


def previous_row(x, end):
    return jnp.where(rows_of(x.shape, 0) == 0, end, pltpu.roll(x, 1, 0))


def next_lane(x):
    return pltpu.roll(x, x.shape[1] - 1, 1)


def previous_lane(x):
    return pltpu.roll(x, 1, 1)


def eddy_plane(cells, upper, lower, ends, factors, across):
    along = 1 - across
    scaled = [0.25 * factors[k] for k in range(3)]
    carried = [0.125 * cells[k] for k in range(3)]
    up = [scaled[k] - carried[k] for k in range(3)]
    down = [scaled[k] + carried[k] for k in range(3)]
    lanes = rows_of(cells[0].shape, 1)
    up[2] = jnp.where(lanes == C3 - 1, 0.0, up[2])
    down[2] = jnp.where(lanes == 0, 0.0, down[2])
    own = 1.0 - 2.0 * (scaled[0] + scaled[1] + scaled[2])
    results = []
    for v in range(NV):
        cell = cells[v]
        low_end, high_end = ends[v]
        result = own * cell + up[across] * upper[v] + down[across] * lower[v]
        result += up[along] * next_row(cell, high_end) + down[along] * previous_row(cell, low_end)
        result += up[2] * next_lane(cell) + down[2] * previous_lane(cell)
        results.append(result)
    return results


def acoustic_plane(cells, upper, lower, ends, factors, across, source):
    along = 1 - across
    lanes = rows_of(cells[0].shape, 1)
    scaled = [0.125 * factors[k] for k in range(3)]
    change = [[None] * NV for _ in range(3)]
    for v in range(NV):
        cell = cells[v]
        low_end, high_end = ends[v]
        change[across][v] = upper[v] - lower[v]
        change[along][v] = next_row(cell, high_end) - previous_row(cell, low_end)
        change[2][v] = jnp.where(lanes == C3 - 1, 0.0, next_lane(cell)) - jnp.where(
            lanes == 0, 0.0, previous_lane(cell)
        )
    results = []
    for v in range(NV):
        if v == 0:
            coupling = change[0][1] + change[1][2] + change[2][3]
        else:
            coupling = change[v - 1][0]
        result = cells[v] - 0.125 * coupling
        for k in range(3):
            result -= scaled[k] * change[k][v]
        if source is not None:
            result += 0.25 * source[v]
        results.append(result)
    return results


def plane_step(acoustic, cells, upper, lower, ends, factors, across, source):
    if acoustic:
        return acoustic_plane(cells, upper, lower, ends, factors, across, source)
    return eddy_plane(cells, upper, lower, ends, factors, across)


def pack_slabs(low_q, high_q, low_c, high_c, low_s, high_s, low_out, high_out):
    for v in range(NV):
        low_out[NEAR + v] = low_q[0, v, 0].astype(BF16)
        low_out[FAR + v] = low_q[0, v, 1].astype(BF16)
        high_out[NEAR + v] = high_q[0, v, 1].astype(BF16)
        high_out[FAR + v] = high_q[0, v, 0].astype(BF16)
        low_out[SOURCE + v] = low_s[v, 0].astype(BF16)
        high_out[SOURCE + v] = high_s[v, 1].astype(BF16)
    for k in range(3):
        low_out[COEF + k] = low_c[0, k, 0].astype(BF16)
        high_out[COEF + k] = high_c[0, k, 1].astype(BF16)


def pack_sectors(q, c, s, below, above, low_out, high_out):
    def column(ref, component, j):
        return ref[component, :, j, :].astype(BF16)

    for v in range(NV):
        low_out[NEAR + v] = column(q, v, 0)
        low_out[FAR + v] = column(q, v, 1)
        high_out[NEAR + v] = column(q, v, C2 - 1)
        high_out[FAR + v] = column(q, v, C2 - 2)
        low_out[SOURCE + v] = column(s, v, 0)
        high_out[SOURCE + v] = column(s, v, C2 - 1)
    for k in range(3):
        low_out[COEF + k] = column(c, k, 0)
        high_out[COEF + k] = column(c, k, C2 - 1)
    for out, j in ((low_out, 0), (high_out, C2 - 1)):
        rows = []
        for v in range(NV):
            rows.append(below[NEAR + v].astype(F32)[j : j + 1])
            rows.append(above[NEAR + v].astype(F32)[j : j + 1])
        rows.append(jnp.zeros((C1 - 2 * NV, C3), F32))
        out[CORNER] = jnp.concatenate(rows, axis=0).astype(BF16)


def first_step(where, ids, q, c, s, below, above, left, right, stepped, rims, packed, sides, stage):
    for side, message in enumerate((left, right)):
        for v in range(NV):
            sides[side, v] = message[NEAR + v].astype(F32)

    def fields_of(message, start, count=NV):
        return [message[start + v].astype(F32) for v in range(count)]

    def run(acoustic):
        corners = [message[CORNER].astype(F32) for message in (left, right)]

        for side, message in enumerate((left, right)):
            near = [sides[side, v] for v in range(NV)]
            far = fields_of(message, FAR)
            own = [q[v, :, 0 if side == 0 else C2 - 1, :] for v in range(NV)]
            ends = [
                (corners[side][2 * v : 2 * v + 1], corners[side][2 * v + 1 : 2 * v + 2])
                for v in range(NV)
            ]
            upper, lower = (own, far) if side == 0 else (far, own)
            source = fields_of(message, SOURCE) if acoustic else None
            results = plane_step(
                acoustic, near, upper, lower, ends, fields_of(message, COEF, 3), 1, source
            )
            for v in range(NV):
                rims[side, v] = results[v]

        for side, message in enumerate((below, above)):
            near = fields_of(message, NEAR)
            far = fields_of(message, FAR)
            own = [q[v, 0 if side == 0 else C1 - 1] for v in range(NV)]
            ends = [
                (
                    corners[0][2 * v + side : 2 * v + side + 1],
                    corners[1][2 * v + side : 2 * v + side + 1],
                )
                for v in range(NV)
            ]
            upper, lower = (own, far) if side == 0 else (far, own)
            source = fields_of(message, SOURCE) if acoustic else None
            results = plane_step(
                acoustic, near, upper, lower, ends, fields_of(message, COEF, 3), 0, source
            )
            inside = where[1] > 0 if side == 0 else where[1] < where[2] - 1
            for v in range(NV):
                rims[2 + side, v] = jnp.where(inside, results[v], 0.0)

        def row(i, upper, lower):
            cells = [q[v, i] for v in range(NV)]
            ends = [(sides[0, v, pl.ds(i, 1), :], sides[1, v, pl.ds(i, 1), :]) for v in range(NV)]
            factors = [c[k, i] for k in range(3)]
            source = [s[v, i] for v in range(NV)] if acoustic else None
            results = plane_step(acoustic, cells, upper, lower, ends, factors, 0, source)
            for v in range(NV):
                stepped[v, i] = results[v]

        row(0, [q[v, 1] for v in range(NV)], fields_of(below, NEAR))
        row(C1 - 1, fields_of(above, NEAR), [q[v, C1 - 2] for v in range(NV)])

        @pl.loop(1, C1 - 1)
        def _(i):
            row(i, [q[v, i + 1] for v in range(NV)], [q[v, i - 1] for v in range(NV)])

    @pl.when(where[0] == 0)
    def _():
        run(False)

        @pl.loop(0, packed.shape[0] // 2)
        def _(r):
            packed[r] = jnp.zeros(packed.shape[1:], BF16)
            for k in range(CAP):
                block = ids[k, r]
                chosen = jnp.maximum(block, 0)
                i = chosen // (2 * C2)
                j = (chosen // 2) % C2
                for v in range(NV):
                    line = stepped[v, i, pl.ds(j, 1), :]
                    half = jnp.where(chosen % 2 == 0, line[:, :LINE], line[:, LINE:])
                    stage[pl.ds(k * NV + v, 1), :] = jnp.where(block >= 0, half, 0.0)
            packed[packed.shape[0] // 2 + r] = stage[...].astype(BF16)

    @pl.when(where[0] != 0)
    def _():
        run(True)
        packed[...] = jnp.zeros(packed.shape, BF16)


def second_step(where, q, c, rims, out):
    def run(acoustic):
        def row(i, upper, lower):
            cells = [q[v, i] for v in range(NV)]
            ends = [(rims[0, v, pl.ds(i, 1), :], rims[1, v, pl.ds(i, 1), :]) for v in range(NV)]
            factors = [c[k, i] for k in range(3)]
            results = plane_step(acoustic, cells, upper, lower, ends, factors, 0, None)
            for v in range(NV):
                out[v, i] = results[v]

        row(0, [q[v, 1] for v in range(NV)], [rims[2, v] for v in range(NV)])
        row(C1 - 1, [rims[3, v] for v in range(NV)], [q[v, C1 - 2] for v in range(NV)])

        @pl.loop(1, C1 - 1)
        def _(i):
            row(i, [q[v, i + 1] for v in range(NV)], [q[v, i - 1] for v in range(NV)])

    @pl.when(where[0] == 0)
    def _():
        run(False)

    @pl.when(where[0] != 0)
    def _():
        run(True)


def add_source(where, targets, weights, received, blocks, base, out, products, sums):
    @pl.when(where[0] == 0)
    def _():
        out[...] = base[...]

    @pl.when(where[0] != 0)
    def _():
        count = received.shape[0] // 2
        lines = received[0:count].reshape(count * CAP * NV, LINE)
        for w in range(NW):
            products[w] = lax.dot_general(
                lines, blocks[w], (((1,), (1,)), ((), ())), preferred_element_type=F32
            )
        sums[...] = jnp.zeros(sums.shape, F32)

        @pl.loop(0, count)
        def _(a):
            for k in range(CAP):
                target = targets[k, a]
                w = weights[k, a]
                i = target // (2 * C2)
                j = (target // 2) % C2
                half = target % 2
                held = []
                for v in range(NV):
                    added = products[w, pl.ds(a * (CAP * NV) + k * NV + v, 1), :]
                    held.append(sums[half, v, i, pl.ds(j, 1), :] + added)
                for v in range(NV):
                    sums[half, v, i, pl.ds(j, 1), :] = held[v]

        for half in range(2):
            lanes = slice(half * LINE, (half + 1) * LINE)
            out[:, :, :, lanes] = base[:, :, :, lanes] + 0.25 * sums[half]


def shards(fields, coefficients, old_source, weight_blocks, send_ids, target_ids, weight_ids):
    current = fields[0]
    factors = coefficients[0]
    peers = lax.axis_size("sec") * lax.axis_size("ax")
    where = jnp.stack(
        [lax.axis_index("sec"), lax.axis_index("ax"), jnp.int32(lax.axis_size("ax"))]
    ).astype(jnp.int32)

    def struct(*shape, dtype=F32):
        return jax.ShapeDtypeStruct(shape, dtype)

    message = struct(PLANES, C1, C3, dtype=BF16)

    last = C1 // 2 - 1
    slab_specs = []
    for lead in ((1, NV), (1, 3), (NV,)):
        for at in (0, last):
            slab_specs.append(
                pl.BlockSpec(
                    lead + (2, C2, C3),
                    lambda _, at=at, lead=lead: (0,) * len(lead) + (at, 0, 0),
                )
            )
    whole = pl.BlockSpec((PLANES, C2, C3), lambda _: (0, 0, 0))
    low_slab, high_slab = pl.pallas_call(
        pack_slabs,
        grid=(1,),
        in_specs=slab_specs,
        out_specs=[whole, whole],
        out_shape=[message, message],
        name="pack_slabs",
    )(fields, fields, coefficients, coefficients, old_source, old_source)
    below = shift(high_slab, "ax", 1, False)
    above = shift(low_slab, "ax", -1, False)

    low_sector, high_sector = pl.pallas_call(
        pack_sectors,
        in_specs=[VMEM] * 5,
        out_specs=[VMEM, VMEM],
        out_shape=[message, message],
        name="pack_sectors",
    )(current, factors, old_source, below, above)
    left = shift(high_sector, "az", 1, True)
    right = shift(low_sector, "az", -1, True)

    stepped, rims, packed = pl.pallas_call(
        first_step,
        in_specs=[SMEM, SMEM] + [VMEM] * 7,
        out_specs=[VMEM] * 3,
        out_shape=[
            struct(NV, C1, C2, C3),
            struct(4, NV, C1, C3),
            struct(peers, CAP * NV, LINE, dtype=BF16),
        ],
        scratch_shapes=[pltpu.VMEM((2, NV, C1, C3), F32), pltpu.VMEM((CAP * NV, LINE), F32)],
        name="first_step",
    )(
        where,
        send_ids[0, 0].T,
        current,
        factors,
        old_source,
        below,
        above,
        left,
        right,
    )
    received = lax.all_to_all(packed, ("sec", "ax"), split_axis=0, concat_axis=0, tiled=True)
    base = pl.pallas_call(
        second_step,
        in_specs=[SMEM] + [VMEM] * 3,
        out_specs=VMEM,
        out_shape=struct(NV, C1, C2, C3),
        name="second_step",
    )(where, stepped, factors, rims)
    advanced = pl.pallas_call(
        add_source,
        in_specs=[SMEM] * 3 + [VMEM] * 3,
        out_specs=VMEM,
        out_shape=struct(NV, C1, C2, C3),
        scratch_shapes=[
            pltpu.VMEM((NW, peers // 2 * CAP * NV, LINE), F32),
            pltpu.VMEM((2, NV, C1, C2, LINE), F32),
        ],
        name="add_source",
    )(where, target_ids[0, 0].T, weight_ids[0, 0].T, received, weight_blocks[0, 0], base)
    return advanced[None]


def solution(mesh):
    return jax.shard_map(
        shards,
        mesh=mesh,
        in_specs=(
            P("sec", None, "ax", "az", None),
            P("sec", None, "ax", "az", None),
            P(None, "ax", "az", None),
            P("ax", "az", None, None, None),
            P("ax", "az", None, None),
            P("ax", "az", None, None),
            P("ax", "az", None, None),
        ),
        out_specs=P("sec", None, "ax", "az", None),
        check_vma=False,
    )
```

```python
import jax
import jax.numpy as jnp
from jax import lax
from jax.experimental import pallas as pl
from jax.experimental.pallas import tpu as pltpu
from jax.sharding import PartitionSpec as P

F32 = jnp.float32
BF16 = jnp.bfloat16
NV = 4
C1 = 16
C2 = 16
C3 = 256
LINE = 128
CAP = 8
NW = 8

NEAR = 0
FAR = 4
COEF = 8
SOURCE = 11
PLANES = 15

VMEM = pl.BlockSpec(memory_space=pltpu.VMEM)
ANY = pl.BlockSpec(memory_space=pl.ANY)
SMEM = pl.BlockSpec(memory_space=pltpu.SMEM)
PARAMS = pltpu.CompilerParams(vmem_limit_bytes=16 << 20)


def off_chip(x):
    return pltpu.with_memory_space_constraint(x, pltpu.HBM)


def shift(x, axis, by, periodic):
    count = lax.axis_size(axis)
    pairs = [(i, (i + by) % count) for i in range(count) if periodic or 0 <= i + by < count]
    return lax.ppermute(x, axis, pairs)


def rows_of(shape, axis):
    return lax.broadcasted_iota(jnp.int32, shape, axis)


def next_row(x, end):
    return jnp.where(rows_of(x.shape, 0) == x.shape[0] - 1, end, pltpu.roll(x, x.shape[0] - 1, 0))


def previous_row(x, end):
    return jnp.where(rows_of(x.shape, 0) == 0, end, pltpu.roll(x, 1, 0))


def next_lane(x):
    return pltpu.roll(x, x.shape[1] - 1, 1)


def previous_lane(x):
    return pltpu.roll(x, 1, 1)


def eddy_plane(cells, upper, lower, ends, factors, across):
    along = 1 - across
    scaled = [0.25 * factors[k] for k in range(3)]
    carried = [0.125 * cells[k] for k in range(3)]
    up = [scaled[k] - carried[k] for k in range(3)]
    down = [scaled[k] + carried[k] for k in range(3)]
    lanes = rows_of(cells[0].shape, 1)
    up[2] = jnp.where(lanes == C3 - 1, 0.0, up[2])
    down[2] = jnp.where(lanes == 0, 0.0, down[2])
    own = 1.0 - 2.0 * (scaled[0] + scaled[1] + scaled[2])
    results = []
    for v in range(NV):
        cell = cells[v]
        low_end, high_end = ends[v]
        result = own * cell + up[across] * upper[v] + down[across] * lower[v]
        result += up[along] * next_row(cell, high_end) + down[along] * previous_row(cell, low_end)
        result += up[2] * next_lane(cell) + down[2] * previous_lane(cell)
        results.append(result)
    return results


def acoustic_plane(cells, upper, lower, ends, factors, across, source):
    along = 1 - across
    lanes = rows_of(cells[0].shape, 1)
    scaled = [0.125 * factors[k] for k in range(3)]
    change = [[None] * NV for _ in range(3)]
    for v in range(NV):
        cell = cells[v]
        low_end, high_end = ends[v]
        change[across][v] = upper[v] - lower[v]
        change[along][v] = next_row(cell, high_end) - previous_row(cell, low_end)
        change[2][v] = jnp.where(lanes == C3 - 1, 0.0, next_lane(cell)) - jnp.where(
            lanes == 0, 0.0, previous_lane(cell)
        )
    results = []
    for v in range(NV):
        if v == 0:
            coupling = change[0][1] + change[1][2] + change[2][3]
        else:
            coupling = change[v - 1][0]
        result = cells[v] - 0.125 * coupling
        for k in range(3):
            result -= scaled[k] * change[k][v]
        if source is not None:
            result += 0.25 * source[v]
        results.append(result)
    return results


def plane_step(acoustic, cells, upper, lower, ends, factors, across, source):
    if acoustic:
        return acoustic_plane(cells, upper, lower, ends, factors, across, source)
    return eddy_plane(cells, upper, lower, ends, factors, across)


def column(ref, component, j):
    return ref[component, :, j, :]


def pack_halos(q, c, s, low_slab, high_slab, low_sector, high_sector, cells, factors, source, done):
    parts = []
    for v in range(NV):
        parts.append((q.at[v], cells.at[v]))
    for k in range(3):
        parts.append((c.at[k], factors.at[k]))
    for v in range(NV):
        parts.append((s.at[v], source.at[v]))
    copies = [pltpu.make_async_copy(*part, done.at[n]) for n, part in enumerate(parts)]
    for copy in copies:
        copy.start()
    for n, copy in enumerate(copies):
        copy.wait()
        if n < NV:
            ref, component, plane = cells, n, NEAR + n
        elif n < NV + 3:
            ref, component, plane = factors, n - NV, COEF + n - NV
        else:
            ref, component, plane = source, n - NV - 3, SOURCE + n - NV - 3
        low_slab[plane] = ref[component, 0].astype(BF16)
        high_slab[plane] = ref[component, C1 - 1].astype(BF16)
        low_sector[plane] = column(ref, component, 0).astype(BF16)
        high_sector[plane] = column(ref, component, C2 - 1).astype(BF16)
        if n < NV:
            low_slab[FAR + n] = ref[component, 1].astype(BF16)
            high_slab[FAR + n] = ref[component, C1 - 2].astype(BF16)
            low_sector[FAR + n] = column(ref, component, 1).astype(BF16)
            high_sector[FAR + n] = column(ref, component, C2 - 2).astype(BF16)


def fields_of(message, start, count=NV):
    return [message[start + v].astype(F32) for v in range(count)]


def step_rows(acoustic, q, c, s, below, above, ends_of, out):
    def row(i, upper, lower):
        cells = [q[v, i] for v in range(NV)]
        factors = [c[k, i] for k in range(3)]
        source = None if s is None else [s[v, i] for v in range(NV)]
        results = plane_step(acoustic, cells, upper, lower, ends_of(i), factors, 0, source)
        for v in range(NV):
            out[v, i] = results[v]

    row(0, [q[v, 1] for v in range(NV)], below)
    row(C1 - 1, above, [q[v, C1 - 2] for v in range(NV)])

    @pl.loop(1, C1 - 1)
    def _(i):
        row(i, [q[v, i + 1] for v in range(NV)], [q[v, i - 1] for v in range(NV)])


def ends_from(sides):
    def ends_of(i):
        return [(sides[0, v, pl.ds(i, 1), :], sides[1, v, pl.ds(i, 1), :]) for v in range(NV)]

    return ends_of


def first_step(ids, q, c, s, below, above, left, right, stepped, packed, sides, stage):
    section = lax.axis_index("sec")
    slab = lax.axis_index("ax")
    slabs = packed.shape[0] // 2
    for side, message in enumerate((left, right)):
        for v in range(NV):
            sides[side, v] = message[NEAR + v].astype(F32)

    def run(acoustic):
        step_rows(
            acoustic,
            q,
            c,
            s if acoustic else None,
            fields_of(below, NEAR),
            fields_of(above, NEAR),
            ends_from(sides),
            stepped,
        )

    @pl.when(section == 0)
    def _():
        run(False)

        @pl.loop(0, slabs)
        def _(r):
            packed[r] = jnp.zeros(packed.shape[1:], BF16)
            for k in range(CAP):
                block = ids[k, r]
                chosen = jnp.maximum(block, 0)
                i = chosen // (2 * C2)
                j = (chosen // 2) % C2
                for v in range(NV):
                    line = stepped[v, i, pl.ds(j, 1), :]
                    half = jnp.where(chosen % 2 == 0, line[:, :LINE], line[:, LINE:])
                    stage[pl.ds(k * NV + v, 1), :] = jnp.where(block >= 0, half, 0.0)
            packed[slabs + r] = stage[...].astype(BF16)

    @pl.when(section != 0)
    def _():
        run(True)
        packed[...] = jnp.zeros(packed.shape, BF16)

    def send_corners(peer, i):
        rows = []
        for v in range(NV):
            for side in range(2):
                row = sides[side, v, i : i + 1, :]
                rows += [row[:, :LINE], row[:, LINE:]]
        rows.append(jnp.zeros((CAP * NV - len(rows), LINE), F32))
        packed[section * slabs + peer] = jnp.concatenate(rows, axis=0).astype(BF16)

    @pl.when(slab > 0)
    def _():
        send_corners(slab - 1, 0)

    @pl.when(slab < slabs - 1)
    def _():
        send_corners(slab + 1, C1 - 1)


def second_step(stepped, q, c, below, above, left, right, out, paths, rims):
    section = lax.axis_index("sec")
    slab = lax.axis_index("ax")
    slabs = lax.axis_size("ax")

    def run(acoustic):
        nothing = jnp.zeros((1, C3), F32)
        ends = [(nothing, nothing)] * NV

        def rim(message, across, own, side):
            near = fields_of(message, NEAR)
            far = fields_of(message, FAR)
            upper, lower = (own, far) if side == 0 else (far, own)
            source = fields_of(message, SOURCE) if acoustic else None
            factors = fields_of(message, COEF, 3)
            return plane_step(acoustic, near, upper, lower, ends, factors, across, source)

        for side, message in enumerate((left, right)):
            own = [column(q, v, side * (C2 - 1)) for v in range(NV)]
            results = rim(message, 1, own, side)
            for v in range(NV):
                rims[side, v] = results[v]

        for side, message in enumerate((below, above)):
            own = [q[v, side * (C1 - 1)] for v in range(NV)]
            results = rim(message, 0, own, side)
            inside = slab > 0 if side == 0 else slab < slabs - 1
            for v in range(NV):
                rims[2 + side, v] = jnp.where(inside, results[v], 0.0)

        step_rows(
            acoustic,
            stepped,
            c,
            None,
            [rims[2, v] for v in range(NV)],
            [rims[3, v] for v in range(NV)],
            ends_from(rims),
            out,
        )

        for low in range(2):
            for side in range(2):
                i = low * (C1 - 1)
                j = side * (C2 - 1)
                slab_rim = (below, above)[low]
                sector_rim = (left, right)[side]

                def rim_row(message, plane, at):
                    return message[plane].astype(F32)[at : at + 1]

                if acoustic:
                    paths[low, side, 0:1] = 0.125 * rim_row(sector_rim, COEF, i)
                    paths[low, side, 1:2] = 0.125 * c[1, i, j : j + 1]
                    paths[low, side, 2:3] = 0.125 * rim_row(slab_rim, COEF + 1, j)
                    paths[low, side, 3:4] = 0.125 * c[0, i, j : j + 1]
                else:
                    toward_slab = 0.125 - 0.25 * low
                    toward_sector = 0.125 - 0.25 * side
                    over_sector = 0.25 * c[1, i, j : j + 1]
                    over_sector += toward_sector * stepped[1, i, j : j + 1]
                    over_sector *= 0.25 * rim_row(
                        sector_rim, COEF, i
                    ) + toward_slab * rim_row(sector_rim, NEAR, i)
                    over_slab = 0.25 * c[0, i, j : j + 1]
                    over_slab += toward_slab * stepped[0, i, j : j + 1]
                    over_slab *= 0.25 * rim_row(
                        slab_rim, COEF + 1, j
                    ) + toward_sector * rim_row(slab_rim, NEAR + 1, j)
                    paths[low, side, 0:1] = over_sector + over_slab

    @pl.when(section == 0)
    def _():
        run(False)

    @pl.when(section != 0)
    def _():
        run(True)


def coupled(values, factor, k):
    results = [factor * value for value in values]
    results[0] += 0.125 * values[k + 1]
    results[k + 1] += 0.125 * values[0]
    return results


def add_source(targets, weights, received, blocks, base, paths, out, products, sums, total, done):
    section = lax.axis_index("sec")
    slab = lax.axis_index("ax")
    slabs = received.shape[0] // 2

    def corner_terms(acoustic):
        terms = {}
        for low in range(2):
            inside = slab > 0 if low == 0 else slab < slabs - 1
            peer = jnp.clip(slab + 2 * low - 1, 0, slabs - 1)
            rows = received[section * slabs + peer].astype(F32)
            rows = jnp.where(inside, rows, 0.0)
            for side in range(2):
                corner = []
                for v in range(NV):
                    at = 2 * (2 * v + side)
                    corner.append(
                        jnp.concatenate([rows[at : at + 1], rows[at + 1 : at + 2]], axis=1)
                    )
                if not acoustic:
                    terms[low, side] = [paths[low, side, 0:1] * corner[v] for v in range(NV)]
                    continue
                sign = 1.0 if low == side else -1.0
                factors = [paths[low, side, n : n + 1] for n in range(4)]
                over_sector = coupled(coupled(corner, factors[0], 0), factors[1], 1)
                over_slab = coupled(coupled(corner, factors[2], 1), factors[3], 0)
                terms[low, side] = [sign * (a + b) for a, b in zip(over_sector, over_slab)]
        return terms

    def finish(acoustic):
        terms = corner_terms(acoustic)
        copies = []
        for v in range(NV):
            if acoustic:
                for half in range(2):
                    lanes = slice(half * LINE, (half + 1) * LINE)
                    total[v, :, :, lanes] = base[v, :, :, lanes] + 0.25 * sums[half, v]
            else:
                total[v] = base[v]
            for (low, side), term in terms.items():
                j = side * (C2 - 1)
                total[v, low * (C1 - 1), j : j + 1, :] += term[v]
            copies.append(pltpu.make_async_copy(total.at[v], out.at[v], done.at[v]))
            copies[-1].start()
        for copy in copies:
            copy.wait()

    @pl.when(section == 0)
    def _():
        finish(False)

    @pl.when(section != 0)
    def _():
        lines = received[0:slabs].reshape(slabs * CAP * NV, LINE)
        for w in range(NW):
            products[w] = lax.dot_general(
                lines, blocks[w], (((1,), (1,)), ((), ())), preferred_element_type=F32
            )
        sums[...] = jnp.zeros(sums.shape, F32)

        @pl.loop(0, slabs)
        def _(a):
            for k in range(CAP):
                target = targets[k, a]
                w = weights[k, a]
                i = target // (2 * C2)
                j = (target // 2) % C2
                half = target % 2
                held = []
                for v in range(NV):
                    added = products[w, pl.ds(a * (CAP * NV) + k * NV + v, 1), :]
                    held.append(sums[half, v, i, pl.ds(j, 1), :] + added)
                for v in range(NV):
                    sums[half, v, i, pl.ds(j, 1), :] = held[v]

        finish(True)


def shards(fields, coefficients, old_source, weight_blocks, send_ids, target_ids, weight_ids):
    current = fields[0]
    factors = coefficients[0]
    peers = lax.axis_size("sec") * lax.axis_size("ax")
    message = jax.ShapeDtypeStruct((PLANES, C1, C3), BF16)
    field = jax.ShapeDtypeStruct((NV, C1, C2, C3), F32)
    cells = pltpu.VMEM((NV, C1, C2, C3), F32)

    low_slab, high_slab, low_sector, high_sector = pl.pallas_call(
        pack_halos,
        in_specs=[ANY] * 3,
        out_specs=[VMEM] * 4,
        out_shape=[message] * 4,
        scratch_shapes=[
            cells,
            pltpu.VMEM((3, C1, C2, C3), F32),
            cells,
            pltpu.SemaphoreType.DMA((2 * NV + 3,)),
        ],
        compiler_params=PARAMS,
        name="pack_halos",
    )(off_chip(current), off_chip(factors), off_chip(old_source))
    below = shift(high_slab, "ax", 1, False)
    above = shift(low_slab, "ax", -1, False)
    left = shift(high_sector, "az", 1, True)
    right = shift(low_sector, "az", -1, True)

    stepped, packed = pl.pallas_call(
        first_step,
        in_specs=[SMEM] + [VMEM] * 7,
        out_specs=[VMEM] * 2,
        out_shape=[field, pltpu.HBM((peers, CAP * NV, LINE), BF16)],
        scratch_shapes=[pltpu.VMEM((2, NV, C1, C3), F32), pltpu.VMEM((CAP * NV, LINE), F32)],
        compiler_params=PARAMS,
        name="first_step",
    )(
        send_ids[0, 0].T,
        current,
        factors,
        old_source,
        below,
        above,
        left,
        right,
    )
    received = lax.all_to_all(packed, ("sec", "ax"), split_axis=0, concat_axis=0, tiled=True)
    base, paths = pl.pallas_call(
        second_step,
        in_specs=[VMEM] * 7,
        out_specs=[VMEM] * 2,
        out_shape=[
            field,
            jax.ShapeDtypeStruct((2, 2, 8, C3), F32),
        ],
        scratch_shapes=[pltpu.VMEM((4, NV, C1, C3), F32)],
        compiler_params=PARAMS,
        name="second_step",
    )(stepped, off_chip(current), off_chip(factors), below, above, left, right)
    advanced = pl.pallas_call(
        add_source,
        in_specs=[SMEM] * 2 + [VMEM] * 4,
        out_specs=ANY,
        out_shape=jax.ShapeDtypeStruct((NV, C1, C2, C3), F32),
        scratch_shapes=[
            pltpu.VMEM((NW, peers // 2 * CAP * NV, LINE), F32),
            pltpu.VMEM((2, NV, C1, C2, LINE), F32),
            cells,
            pltpu.SemaphoreType.DMA((NV,)),
        ],
        compiler_params=PARAMS,
        name="add_source",
    )(
        target_ids[0, 0].T,
        weight_ids[0, 0].T,
        received,
        weight_blocks[0, 0],
        base,
        paths,
    )
    return advanced[None]


def solution(mesh):
    return jax.shard_map(
        shards,
        mesh=mesh,
        in_specs=(
            P("sec", None, "ax", "az", None),
            P("sec", None, "ax", "az", None),
            P(None, "ax", "az", None),
            P("ax", "az", None, None, None),
            P("ax", "az", None, None),
            P("ax", "az", None, None),
            P("ax", "az", None, None),
        ),
        out_specs=P("sec", None, "ax", "az", None),
        check_vma=False,
    )
```

```python
import jax
import jax.numpy as jnp
from jax import lax
from jax.experimental import pallas as pl
from jax.experimental.pallas import tpu as pltpu
from jax.sharding import PartitionSpec as P

F32 = jnp.float32
BF16 = jnp.bfloat16
NV = 4
C1 = 16
C2 = 16
C3 = 256
LINE = 128
CAP = 8
NW = 8

NEAR = 0
FAR = 4
COEF = 8
SOURCE = 11
PLANES = 15

VMEM = pl.BlockSpec(memory_space=pltpu.VMEM)
ANY = pl.BlockSpec(memory_space=pl.ANY)
SMEM = pl.BlockSpec(memory_space=pltpu.SMEM)
PARAMS = pltpu.CompilerParams(vmem_limit_bytes=16 << 20)


def off_chip(x):
    return pltpu.with_memory_space_constraint(x, pltpu.HBM)


def shift(x, axis, by, periodic):
    count = lax.axis_size(axis)
    pairs = [(i, (i + by) % count) for i in range(count) if periodic or 0 <= i + by < count]
    return lax.ppermute(x, axis, pairs)


def rows_of(shape, axis):
    return lax.broadcasted_iota(jnp.int32, shape, axis)


def next_row(x, end):
    return jnp.where(rows_of(x.shape, 0) == x.shape[0] - 1, end, pltpu.roll(x, x.shape[0] - 1, 0))


def previous_row(x, end):
    return jnp.where(rows_of(x.shape, 0) == 0, end, pltpu.roll(x, 1, 0))


def next_lane(x):
    return pltpu.roll(x, x.shape[1] - 1, 1)


def previous_lane(x):
    return pltpu.roll(x, 1, 1)


def eddy_plane(cells, upper, lower, ends, factors, across):
    along = 1 - across
    scaled = [0.25 * factors[k] for k in range(3)]
    carried = [0.125 * cells[k] for k in range(3)]
    up = [scaled[k] - carried[k] for k in range(3)]
    down = [scaled[k] + carried[k] for k in range(3)]
    lanes = rows_of(cells[0].shape, 1)
    up[2] = jnp.where(lanes == C3 - 1, 0.0, up[2])
    down[2] = jnp.where(lanes == 0, 0.0, down[2])
    own = 1.0 - 2.0 * (scaled[0] + scaled[1] + scaled[2])
    results = []
    for v in range(NV):
        cell = cells[v]
        low_end, high_end = ends[v]
        result = own * cell + up[across] * upper[v] + down[across] * lower[v]
        result += up[along] * next_row(cell, high_end) + down[along] * previous_row(cell, low_end)
        result += up[2] * next_lane(cell) + down[2] * previous_lane(cell)
        results.append(result)
    return results


def acoustic_plane(cells, upper, lower, ends, factors, across, source):
    along = 1 - across
    lanes = rows_of(cells[0].shape, 1)
    scaled = [0.125 * factors[k] for k in range(3)]
    change = [[None] * NV for _ in range(3)]
    for v in range(NV):
        cell = cells[v]
        low_end, high_end = ends[v]
        change[across][v] = upper[v] - lower[v]
        change[along][v] = next_row(cell, high_end) - previous_row(cell, low_end)
        change[2][v] = jnp.where(lanes == C3 - 1, 0.0, next_lane(cell)) - jnp.where(
            lanes == 0, 0.0, previous_lane(cell)
        )
    results = []
    for v in range(NV):
        if v == 0:
            coupling = change[0][1] + change[1][2] + change[2][3]
        else:
            coupling = change[v - 1][0]
        result = cells[v] - 0.125 * coupling
        for k in range(3):
            result -= scaled[k] * change[k][v]
        if source is not None:
            result += 0.25 * source[v]
        results.append(result)
    return results


def plane_step(acoustic, cells, upper, lower, ends, factors, across, source):
    if acoustic:
        return acoustic_plane(cells, upper, lower, ends, factors, across, source)
    return eddy_plane(cells, upper, lower, ends, factors, across)


def column(ref, component, j):
    return ref[component, :, j, :]


def pack_halos(q, c, s, low_slab, high_slab, low_sector, high_sector, cells, factors, source, done):
    parts = []
    for v in range(NV):
        parts.append((q.at[v], cells.at[v]))
    for k in range(3):
        parts.append((c.at[k], factors.at[k]))
    for v in range(NV):
        parts.append((s.at[v], source.at[v]))
    copies = [pltpu.make_async_copy(*part, done.at[n]) for n, part in enumerate(parts)]
    for copy in copies:
        copy.start()
    for n, copy in enumerate(copies):
        copy.wait()
        if n < NV:
            ref, component, plane = cells, n, NEAR + n
        elif n < NV + 3:
            ref, component, plane = factors, n - NV, COEF + n - NV
        else:
            ref, component, plane = source, n - NV - 3, SOURCE + n - NV - 3
        low_slab[plane] = ref[component, 0].astype(BF16)
        high_slab[plane] = ref[component, C1 - 1].astype(BF16)
        low_sector[plane] = column(ref, component, 0).astype(BF16)
        high_sector[plane] = column(ref, component, C2 - 1).astype(BF16)
        if n < NV:
            low_slab[FAR + n] = ref[component, 1].astype(BF16)
            high_slab[FAR + n] = ref[component, C1 - 2].astype(BF16)
            low_sector[FAR + n] = column(ref, component, 1).astype(BF16)
            high_sector[FAR + n] = column(ref, component, C2 - 2).astype(BF16)


def fields_of(message, start, count=NV):
    return [message[start + v].astype(F32) for v in range(count)]


def step_rows(acoustic, q, c, s, below, above, ends_of, out):
    def row(i, upper, lower):
        cells = [q[v, i] for v in range(NV)]
        factors = [c[k, i] for k in range(3)]
        source = None if s is None else [s[v, i] for v in range(NV)]
        results = plane_step(acoustic, cells, upper, lower, ends_of(i), factors, 0, source)
        for v in range(NV):
            out[v, i] = results[v]

    row(0, [q[v, 1] for v in range(NV)], below)
    row(C1 - 1, above, [q[v, C1 - 2] for v in range(NV)])

    @pl.loop(1, C1 - 1)
    def _(i):
        row(i, [q[v, i + 1] for v in range(NV)], [q[v, i - 1] for v in range(NV)])


def no_ends(i):
    nothing = jnp.zeros((1, C3), F32)
    return [(nothing, nothing)] * NV


def inner_step(q, c, s, out):
    section = lax.axis_index("sec")
    nothing = [jnp.zeros((C2, C3), F32)] * NV

    @pl.when(section == 0)
    def _():
        step_rows(False, q, c, None, nothing, nothing, no_ends, out)

    @pl.when(section != 0)
    def _():
        step_rows(True, q, c, s, nothing, nothing, no_ends, out)


def coupled(values, factor, k):
    results = [factor * value for value in values]
    results[0] += 0.125 * values[k + 1]
    results[k + 1] += 0.125 * values[0]
    return results


def border_terms(acoustic, near, flow, factor, k, side):
    sign = 1.0 - 2.0 * side
    if acoustic:
        return [sign * term for term in coupled(near, 0.125 * factor, k)]
    weight = 0.25 * factor + (sign * 0.125) * flow
    return [weight * value for value in near]


def first_step(ids, inner, q, c, below, above, left, right, stepped, packed, sides):
    section = lax.axis_index("sec")
    slab = lax.axis_index("ax")
    slabs = packed.shape[0] // 2
    for side, message in enumerate((left, right)):
        for v in range(NV):
            sides[side, v] = message[NEAR + v].astype(F32)

    def add_borders(acoustic):
        for side, message in enumerate((below, above)):
            i = side * (C1 - 1)
            near = fields_of(message, NEAR)
            terms = border_terms(acoustic, near, q[0, i], c[0, i], 0, side)
            for v in range(NV):
                stepped[v, i] += terms[v]
        for i in range(C1):
            for side in range(2):
                j = side * (C2 - 1)
                near = [sides[side, v, i : i + 1, :] for v in range(NV)]
                flow = q[1, i, j : j + 1, :]
                factor = c[1, i, j : j + 1, :]
                terms = border_terms(acoustic, near, flow, factor, 1, side)
                for v in range(NV):
                    stepped[v, i, j : j + 1, :] += terms[v]

    @pl.when(section == 0)
    def _():
        add_borders(False)

        listed = ids[...]
        columns = [listed[:, r : r + 1] for r in range(slabs)]
        lanes = rows_of((CAP, C1 * C2), 1)
        chosen = [jnp.where(lanes == (column >> 1), 1.0, 0.0) for column in columns]
        chosen = jnp.concatenate(chosen, axis=0).astype(BF16)
        picked = []
        for v in range(NV):
            cells = stepped[v].astype(BF16).reshape(C1 * C2, C3)
            picked.append(jnp.dot(chosen, cells, preferred_element_type=F32))
        for r in range(slabs):
            odd = jnp.broadcast_to(columns[r] & 1, (CAP, LINE)) == 1
            rows = []
            for v in range(NV):
                both = picked[v][r * CAP : (r + 1) * CAP]
                rows.append(jnp.where(odd, both[:, LINE:], both[:, :LINE]))
            packed[slabs + r] = jnp.concatenate(rows, axis=0).astype(BF16)

    @pl.when(section != 0)
    def _():
        add_borders(True)

    def send_corners(peer, i):
        rows = []
        for v in range(NV):
            for side in range(2):
                row = sides[side, v, i : i + 1, :]
                rows += [row[:, :LINE], row[:, LINE:]]
        rows.append(jnp.zeros((CAP * NV - len(rows), LINE), F32))
        packed[section * slabs + peer] = jnp.concatenate(rows, axis=0).astype(BF16)

    @pl.when(slab > 0)
    def _():
        send_corners(slab - 1, 0)

    @pl.when(slab < slabs - 1)
    def _():
        send_corners(slab + 1, C1 - 1)


def ends_from(sides):
    def ends_of(i):
        return [(sides[0, v, pl.ds(i, 1), :], sides[1, v, pl.ds(i, 1), :]) for v in range(NV)]

    return ends_of


def second_step(stepped, q, c, below, above, left, right, out, paths, rims):
    section = lax.axis_index("sec")
    slab = lax.axis_index("ax")
    slabs = lax.axis_size("ax")

    def run(acoustic):
        nothing = jnp.zeros((1, C3), F32)
        ends = [(nothing, nothing)] * NV

        def rim(message, across, own, side):
            near = fields_of(message, NEAR)
            far = fields_of(message, FAR)
            upper, lower = (own, far) if side == 0 else (far, own)
            source = fields_of(message, SOURCE) if acoustic else None
            factors = fields_of(message, COEF, 3)
            return plane_step(acoustic, near, upper, lower, ends, factors, across, source)

        for side, message in enumerate((left, right)):
            own = [column(q, v, side * (C2 - 1)) for v in range(NV)]
            results = rim(message, 1, own, side)
            for v in range(NV):
                rims[side, v] = results[v]

        for side, message in enumerate((below, above)):
            own = [q[v, side * (C1 - 1)] for v in range(NV)]
            results = rim(message, 0, own, side)
            inside = slab > 0 if side == 0 else slab < slabs - 1
            for v in range(NV):
                rims[2 + side, v] = jnp.where(inside, results[v], 0.0)

        step_rows(
            acoustic,
            stepped,
            c,
            None,
            [rims[2, v] for v in range(NV)],
            [rims[3, v] for v in range(NV)],
            ends_from(rims),
            out,
        )

        for low in range(2):
            for side in range(2):
                i = low * (C1 - 1)
                j = side * (C2 - 1)
                slab_rim = (below, above)[low]
                sector_rim = (left, right)[side]

                def rim_row(message, plane, at):
                    return message[plane].astype(F32)[at : at + 1]

                if acoustic:
                    paths[low, side, 0:1] = 0.125 * rim_row(sector_rim, COEF, i)
                    paths[low, side, 1:2] = 0.125 * c[1, i, j : j + 1]
                    paths[low, side, 2:3] = 0.125 * rim_row(slab_rim, COEF + 1, j)
                    paths[low, side, 3:4] = 0.125 * c[0, i, j : j + 1]
                else:
                    toward_slab = 0.125 - 0.25 * low
                    toward_sector = 0.125 - 0.25 * side
                    over_sector = 0.25 * c[1, i, j : j + 1]
                    over_sector += toward_sector * stepped[1, i, j : j + 1]
                    over_sector *= 0.25 * rim_row(
                        sector_rim, COEF, i
                    ) + toward_slab * rim_row(sector_rim, NEAR, i)
                    over_slab = 0.25 * c[0, i, j : j + 1]
                    over_slab += toward_slab * stepped[0, i, j : j + 1]
                    over_slab *= 0.25 * rim_row(
                        slab_rim, COEF + 1, j
                    ) + toward_sector * rim_row(slab_rim, NEAR + 1, j)
                    paths[low, side, 0:1] = over_sector + over_slab

    @pl.when(section == 0)
    def _():
        run(False)

    @pl.when(section != 0)
    def _():
        run(True)


def add_source(targets, weights, received, blocks, base, paths, out, total, done):
    section = lax.axis_index("sec")
    slab = lax.axis_index("ax")
    slabs = received.shape[0] // 2

    def corner_terms(acoustic):
        terms = {}
        for low in range(2):
            inside = slab > 0 if low == 0 else slab < slabs - 1
            peer = jnp.clip(slab + 2 * low - 1, 0, slabs - 1)
            rows = received[section * slabs + peer].astype(F32)
            rows = jnp.where(inside, rows, 0.0)
            for side in range(2):
                corner = []
                for v in range(NV):
                    at = 2 * (2 * v + side)
                    corner.append(
                        jnp.concatenate([rows[at : at + 1], rows[at + 1 : at + 2]], axis=1)
                    )
                if not acoustic:
                    terms[low, side] = [paths[low, side, 0:1] * corner[v] for v in range(NV)]
                    continue
                sign = 1.0 if low == side else -1.0
                factors = [paths[low, side, n : n + 1] for n in range(4)]
                over_sector = coupled(coupled(corner, factors[0], 0), factors[1], 1)
                over_slab = coupled(coupled(corner, factors[2], 1), factors[3], 0)
                terms[low, side] = [sign * (a + b) for a, b in zip(over_sector, over_slab)]
        return terms

    def finish(acoustic, added):
        terms = corner_terms(acoustic)
        copies = []
        for v in range(NV):
            if acoustic:
                for half in range(2):
                    lanes = slice(half * LINE, (half + 1) * LINE)
                    part = added[half][:, v * LINE : (v + 1) * LINE].reshape(C1, C2, LINE)
                    total[v, :, :, lanes] = base[v, :, :, lanes] + part
            else:
                total[v] = base[v]
            for (low, side), term in terms.items():
                j = side * (C2 - 1)
                total[v, low * (C1 - 1), j : j + 1, :] += term[v]
            copies.append(pltpu.make_async_copy(total.at[v], out.at[v], done.at[v]))
            copies[-1].start()
        for copy in copies:
            copy.wait()

    @pl.when(section == 0)
    def _():
        finish(False, None)

    @pl.when(section != 0)
    def _():
        kinds = weights[...]
        masks = []
        for a in range(slabs):
            kind = jnp.broadcast_to(kinds[:, a : a + 1], (CAP, LINE))
            masks.append(jnp.concatenate([kind] * NV, axis=0))
        placed = []
        for w in range(NW):
            parts = []
            for a in range(slabs):
                parts.append(jnp.where(masks[a] == w, 1.0, 0.0).astype(BF16) * received[a])
            placed.append(jnp.concatenate(parts, axis=0))
        placed = jnp.concatenate(placed, axis=1)
        stacked = jnp.concatenate([blocks[w] for w in range(NW)], axis=1)
        products = lax.dot_general(
            placed, stacked, (((1,), (1,)), ((), ())), preferred_element_type=F32
        )
        lines = []
        for v in range(NV):
            rows = []
            for a in range(slabs):
                start = (a * NV + v) * CAP
                rows.append(products[start : start + CAP])
            lines.append(jnp.concatenate(rows, axis=0))
        lines = jnp.concatenate(lines, axis=1)
        high = lines.astype(BF16)
        low = (lines - high.astype(F32)).astype(BF16)
        lines = jnp.concatenate([high, low], axis=0)
        wanted = jnp.concatenate([targets[...]] * 2, axis=1)
        added = []
        for half in range(2):
            here = 2 * rows_of((C1 * C2, lines.shape[0]), 0) + half
            chosen = jnp.where(here == wanted, 0.25, 0.0).astype(BF16)
            added.append(jnp.dot(chosen, lines, preferred_element_type=F32))
        finish(True, added)


def shards(fields, coefficients, old_source, weight_blocks, send_ids, target_ids, weight_ids):
    current = fields[0]
    factors = coefficients[0]
    peers = lax.axis_size("sec") * lax.axis_size("ax")
    message = jax.ShapeDtypeStruct((PLANES, C1, C3), BF16)
    field = jax.ShapeDtypeStruct((NV, C1, C2, C3), F32)
    cells = pltpu.VMEM((NV, C1, C2, C3), F32)

    low_slab, high_slab, low_sector, high_sector = pl.pallas_call(
        pack_halos,
        in_specs=[ANY] * 3,
        out_specs=[VMEM] * 4,
        out_shape=[message] * 4,
        scratch_shapes=[
            cells,
            pltpu.VMEM((3, C1, C2, C3), F32),
            cells,
            pltpu.SemaphoreType.DMA((2 * NV + 3,)),
        ],
        compiler_params=PARAMS,
        name="pack_halos",
    )(off_chip(current), off_chip(factors), off_chip(old_source))
    below = shift(high_slab, "ax", 1, False)
    above = shift(low_slab, "ax", -1, False)
    left = shift(high_sector, "az", 1, True)
    right = shift(low_sector, "az", -1, True)

    inner = pl.pallas_call(
        inner_step,
        in_specs=[VMEM] * 3,
        out_specs=VMEM,
        out_shape=field,
        compiler_params=PARAMS,
        name="inner_step",
    )(current, factors, old_source)
    stepped, packed = pl.pallas_call(
        first_step,
        in_specs=[VMEM] * 8,
        out_specs=[VMEM] * 2,
        out_shape=[field, pltpu.HBM((peers, CAP * NV, LINE), BF16)],
        input_output_aliases={1: 0},
        scratch_shapes=[pltpu.VMEM((2, NV, C1, C3), F32)],
        compiler_params=PARAMS,
        name="first_step",
    )(send_ids[0, 0].T, inner, current, factors, below, above, left, right)
    received = lax.all_to_all(packed, ("sec", "ax"), split_axis=0, concat_axis=0, tiled=True)
    base, paths = pl.pallas_call(
        second_step,
        in_specs=[VMEM] * 7,
        out_specs=[VMEM] * 2,
        out_shape=[
            field,
            jax.ShapeDtypeStruct((2, 2, 8, C3), F32),
        ],
        scratch_shapes=[pltpu.VMEM((4, NV, C1, C3), F32)],
        compiler_params=PARAMS,
        name="second_step",
    )(stepped, off_chip(current), off_chip(factors), below, above, left, right)
    advanced = pl.pallas_call(
        add_source,
        in_specs=[VMEM] * 6,
        out_specs=ANY,
        out_shape=jax.ShapeDtypeStruct((NV, C1, C2, C3), F32),
        scratch_shapes=[cells, pltpu.SemaphoreType.DMA((NV,))],
        compiler_params=PARAMS,
        name="add_source",
    )(
        target_ids.reshape(1, -1),
        weight_ids[0, 0].T,
        received,
        weight_blocks[0, 0],
        base,
        paths,
    )
    return advanced[None]


def solution(mesh):
    return jax.shard_map(
        shards,
        mesh=mesh,
        in_specs=(
            P("sec", None, "ax", "az", None),
            P("sec", None, "ax", "az", None),
            P(None, "ax", "az", None),
            P("ax", "az", None, None, None),
            P("ax", "az", None, None),
            P("ax", "az", None, None),
            P("ax", "az", None, None),
        ),
        out_specs=P("sec", None, "ax", "az", None),
        check_vma=False,
    )
```

```python
import jax
import jax.numpy as jnp
from jax import lax
from jax.experimental import pallas as pl
from jax.experimental.pallas import tpu as pltpu
from jax.sharding import PartitionSpec as P

F32 = jnp.float32
BF16 = jnp.bfloat16
NV = 4
C1 = 16
C2 = 16
C3 = 256
LINE = 128
CAP = 8
NW = 8

NEAR = 0
FAR = 4
COEF = 8
SOURCE = 11
PLANES = 15

VMEM = pl.BlockSpec(memory_space=pltpu.VMEM)
ANY = pl.BlockSpec(memory_space=pl.ANY)
SMEM = pl.BlockSpec(memory_space=pltpu.SMEM)
PARAMS = pltpu.CompilerParams(vmem_limit_bytes=16 << 20)


def off_chip(x):
    return pltpu.with_memory_space_constraint(x, pltpu.HBM)


def shift(x, axis, by, periodic):
    count = lax.axis_size(axis)
    pairs = [(i, (i + by) % count) for i in range(count) if periodic or 0 <= i + by < count]
    return lax.ppermute(x, axis, pairs)


def rows_of(shape, axis):
    return lax.broadcasted_iota(jnp.int32, shape, axis)


def next_row(x, end):
    return jnp.where(rows_of(x.shape, 0) == x.shape[0] - 1, end, pltpu.roll(x, x.shape[0] - 1, 0))


def previous_row(x, end):
    return jnp.where(rows_of(x.shape, 0) == 0, end, pltpu.roll(x, 1, 0))


def next_lane(x):
    return pltpu.roll(x, x.shape[1] - 1, 1)


def previous_lane(x):
    return pltpu.roll(x, 1, 1)


def eddy_plane(cells, upper, lower, ends, factors, across):
    along = 1 - across
    scaled = [0.25 * factors[k] for k in range(3)]
    carried = [0.125 * cells[k] for k in range(3)]
    up = [scaled[k] - carried[k] for k in range(3)]
    down = [scaled[k] + carried[k] for k in range(3)]
    lanes = rows_of(cells[0].shape, 1)
    up[2] = jnp.where(lanes == C3 - 1, 0.0, up[2])
    down[2] = jnp.where(lanes == 0, 0.0, down[2])
    own = 1.0 - 2.0 * (scaled[0] + scaled[1] + scaled[2])
    results = []
    for v in range(NV):
        cell = cells[v]
        low_end, high_end = ends[v]
        result = own * cell + up[across] * upper[v] + down[across] * lower[v]
        result += up[along] * next_row(cell, high_end) + down[along] * previous_row(cell, low_end)
        result += up[2] * next_lane(cell) + down[2] * previous_lane(cell)
        results.append(result)
    return results


def acoustic_plane(cells, upper, lower, ends, factors, across, source):
    along = 1 - across
    lanes = rows_of(cells[0].shape, 1)
    scaled = [0.125 * factors[k] for k in range(3)]
    change = [[None] * NV for _ in range(3)]
    for v in range(NV):
        cell = cells[v]
        low_end, high_end = ends[v]
        change[across][v] = upper[v] - lower[v]
        change[along][v] = next_row(cell, high_end) - previous_row(cell, low_end)
        change[2][v] = jnp.where(lanes == C3 - 1, 0.0, next_lane(cell)) - jnp.where(
            lanes == 0, 0.0, previous_lane(cell)
        )
    results = []
    for v in range(NV):
        if v == 0:
            coupling = change[0][1] + change[1][2] + change[2][3]
        else:
            coupling = change[v - 1][0]
        result = cells[v] - 0.125 * coupling
        for k in range(3):
            result -= scaled[k] * change[k][v]
        if source is not None:
            result += 0.25 * source[v]
        results.append(result)
    return results


def plane_step(acoustic, cells, upper, lower, ends, factors, across, source):
    if acoustic:
        return acoustic_plane(cells, upper, lower, ends, factors, across, source)
    return eddy_plane(cells, upper, lower, ends, factors, across)


def column(ref, component, j):
    return ref[component, :, j, :]


def pack_halos(q, c, s, low_slab, high_slab, low_sector, high_sector, cells, factors, source, done):
    parts = []
    for v in range(NV):
        parts.append((q.at[v], cells.at[v]))
    for k in range(3):
        parts.append((c.at[k], factors.at[k]))
    for v in range(NV):
        parts.append((s.at[v], source.at[v]))
    copies = [pltpu.make_async_copy(*part, done.at[n]) for n, part in enumerate(parts)]
    for copy in copies:
        copy.start()
    for n, copy in enumerate(copies):
        copy.wait()
        if n < NV:
            ref, component, plane = cells, n, NEAR + n
        elif n < NV + 3:
            ref, component, plane = factors, n - NV, COEF + n - NV
        else:
            ref, component, plane = source, n - NV - 3, SOURCE + n - NV - 3
        low_slab[plane] = ref[component, 0].astype(BF16)
        high_slab[plane] = ref[component, C1 - 1].astype(BF16)
        low_sector[plane] = column(ref, component, 0).astype(BF16)
        high_sector[plane] = column(ref, component, C2 - 1).astype(BF16)
        if n < NV:
            low_slab[FAR + n] = ref[component, 1].astype(BF16)
            high_slab[FAR + n] = ref[component, C1 - 2].astype(BF16)
            low_sector[FAR + n] = column(ref, component, 1).astype(BF16)
            high_sector[FAR + n] = column(ref, component, C2 - 2).astype(BF16)


def fields_of(message, start, count=NV):
    return [message[start + v].astype(F32) for v in range(count)]


def step_rows(acoustic, q, c, s, below, above, ends_of, out):
    def row(i, upper, lower):
        cells = [q[v, i] for v in range(NV)]
        factors = [c[k, i] for k in range(3)]
        source = None if s is None else [s[v, i] for v in range(NV)]
        results = plane_step(acoustic, cells, upper, lower, ends_of(i), factors, 0, source)
        for v in range(NV):
            out[v, i] = results[v]

    row(0, [q[v, 1] for v in range(NV)], below)
    row(C1 - 1, above, [q[v, C1 - 2] for v in range(NV)])

    @pl.loop(1, C1 - 1)
    def _(i):
        row(i, [q[v, i + 1] for v in range(NV)], [q[v, i - 1] for v in range(NV)])


def no_ends(i):
    nothing = jnp.zeros((1, C3), F32)
    return [(nothing, nothing)] * NV


def inner_step(q, c, s, out):
    section = lax.axis_index("sec")
    nothing = [jnp.zeros((C2, C3), F32)] * NV

    @pl.when(section == 0)
    def _():
        step_rows(False, q, c, None, nothing, nothing, no_ends, out)

    @pl.when(section != 0)
    def _():
        step_rows(True, q, c, s, nothing, nothing, no_ends, out)


def coupled(values, factor, k):
    results = [factor * value for value in values]
    results[0] += 0.125 * values[k + 1]
    results[k + 1] += 0.125 * values[0]
    return results


def border_terms(acoustic, near, flow, factor, k, side):
    sign = 1.0 - 2.0 * side
    if acoustic:
        return [sign * term for term in coupled(near, 0.125 * factor, k)]
    weight = 0.25 * factor + (sign * 0.125) * flow
    return [weight * value for value in near]


def first_step(ids, inner, q, c, left, right, below, above, stepped, packed, sides):
    section = lax.axis_index("sec")
    slab = lax.axis_index("ax")
    slabs = packed.shape[0] // 2
    for side, message in enumerate((left, right)):
        for v in range(NV):
            sides[side, v] = message[NEAR + v].astype(F32)

    def add_borders(acoustic):
        for side, message in enumerate((below, above)):
            i = side * (C1 - 1)
            near = fields_of(message, NEAR)
            terms = border_terms(acoustic, near, q[0, i], c[0, i], 0, side)
            for v in range(NV):
                stepped[v, i] += terms[v]
        for i in range(C1):
            for side in range(2):
                j = side * (C2 - 1)
                near = [sides[side, v, i : i + 1, :] for v in range(NV)]
                flow = q[1, i, j : j + 1, :]
                factor = c[1, i, j : j + 1, :]
                terms = border_terms(acoustic, near, flow, factor, 1, side)
                for v in range(NV):
                    stepped[v, i, j : j + 1, :] += terms[v]

    @pl.when(section == 0)
    def _():
        add_borders(False)

        listed = ids[...]
        columns = [listed[:, r : r + 1] for r in range(slabs)]
        lanes = rows_of((CAP, C1 * C2), 1)
        chosen = [jnp.where(lanes == (column >> 1), 1.0, 0.0) for column in columns]
        chosen = jnp.concatenate(chosen, axis=0).astype(BF16)
        picked = []
        for v in range(NV):
            cells = stepped[v].astype(BF16).reshape(C1 * C2, C3)
            picked.append(jnp.dot(chosen, cells, preferred_element_type=F32))
        for r in range(slabs):
            odd = jnp.broadcast_to(columns[r] & 1, (CAP, LINE)) == 1
            rows = []
            for v in range(NV):
                both = picked[v][r * CAP : (r + 1) * CAP]
                rows.append(jnp.where(odd, both[:, LINE:], both[:, :LINE]))
            packed[slabs + r] = jnp.concatenate(rows, axis=0).astype(BF16)

    @pl.when(section != 0)
    def _():
        add_borders(True)

    def send_corners(peer, i):
        rows = []
        for v in range(NV):
            for side in range(2):
                row = sides[side, v, i : i + 1, :]
                rows += [row[:, :LINE], row[:, LINE:]]
        rows.append(jnp.zeros((CAP * NV - len(rows), LINE), F32))
        packed[section * slabs + peer] = jnp.concatenate(rows, axis=0).astype(BF16)

    @pl.when(slab > 0)
    def _():
        send_corners(slab - 1, 0)

    @pl.when(slab < slabs - 1)
    def _():
        send_corners(slab + 1, C1 - 1)


def ends_from(sides):
    def ends_of(i):
        return [(sides[0, v, pl.ds(i, 1), :], sides[1, v, pl.ds(i, 1), :]) for v in range(NV)]

    return ends_of


def second_step(stepped, q, c, left, right, below, above, out, paths, rims):
    section = lax.axis_index("sec")
    slab = lax.axis_index("ax")
    slabs = lax.axis_size("ax")

    def run(acoustic):
        nothing = jnp.zeros((1, C3), F32)
        ends = [(nothing, nothing)] * NV

        def rim(message, across, own, side):
            near = fields_of(message, NEAR)
            far = fields_of(message, FAR)
            upper, lower = (own, far) if side == 0 else (far, own)
            source = fields_of(message, SOURCE) if acoustic else None
            factors = fields_of(message, COEF, 3)
            return plane_step(acoustic, near, upper, lower, ends, factors, across, source)

        for side, message in enumerate((left, right)):
            own = [column(q, v, side * (C2 - 1)) for v in range(NV)]
            results = rim(message, 1, own, side)
            for v in range(NV):
                rims[side, v] = results[v]

        for side, message in enumerate((below, above)):
            own = [q[v, side * (C1 - 1)] for v in range(NV)]
            results = rim(message, 0, own, side)
            inside = slab > 0 if side == 0 else slab < slabs - 1
            for v in range(NV):
                rims[2 + side, v] = jnp.where(inside, results[v], 0.0)

        step_rows(
            acoustic,
            stepped,
            c,
            None,
            [rims[2, v] for v in range(NV)],
            [rims[3, v] for v in range(NV)],
            ends_from(rims),
            out,
        )

        for low in range(2):
            for side in range(2):
                i = low * (C1 - 1)
                j = side * (C2 - 1)
                slab_rim = (below, above)[low]
                sector_rim = (left, right)[side]

                def rim_row(message, plane, at):
                    return message[plane].astype(F32)[at : at + 1]

                if acoustic:
                    paths[low, side, 0:1] = 0.125 * rim_row(sector_rim, COEF, i)
                    paths[low, side, 1:2] = 0.125 * c[1, i, j : j + 1]
                    paths[low, side, 2:3] = 0.125 * rim_row(slab_rim, COEF + 1, j)
                    paths[low, side, 3:4] = 0.125 * c[0, i, j : j + 1]
                else:
                    toward_slab = 0.125 - 0.25 * low
                    toward_sector = 0.125 - 0.25 * side
                    over_sector = 0.25 * c[1, i, j : j + 1]
                    over_sector += toward_sector * stepped[1, i, j : j + 1]
                    over_sector *= 0.25 * rim_row(
                        sector_rim, COEF, i
                    ) + toward_slab * rim_row(sector_rim, NEAR, i)
                    over_slab = 0.25 * c[0, i, j : j + 1]
                    over_slab += toward_slab * stepped[0, i, j : j + 1]
                    over_slab *= 0.25 * rim_row(
                        slab_rim, COEF + 1, j
                    ) + toward_sector * rim_row(slab_rim, NEAR + 1, j)
                    paths[low, side, 0:1] = over_sector + over_slab

    @pl.when(section == 0)
    def _():
        run(False)

    @pl.when(section != 0)
    def _():
        run(True)


def add_source(targets, weights, received, blocks, base, paths, out, total, done):
    section = lax.axis_index("sec")
    slab = lax.axis_index("ax")
    slabs = received.shape[0] // 2

    def corner_terms(acoustic):
        terms = {}
        for low in range(2):
            inside = slab > 0 if low == 0 else slab < slabs - 1
            peer = jnp.clip(slab + 2 * low - 1, 0, slabs - 1)
            rows = received[section * slabs + peer].astype(F32)
            rows = jnp.where(inside, rows, 0.0)
            for side in range(2):
                corner = []
                for v in range(NV):
                    at = 2 * (2 * v + side)
                    corner.append(
                        jnp.concatenate([rows[at : at + 1], rows[at + 1 : at + 2]], axis=1)
                    )
                if not acoustic:
                    terms[low, side] = [paths[low, side, 0:1] * corner[v] for v in range(NV)]
                    continue
                sign = 1.0 if low == side else -1.0
                factors = [paths[low, side, n : n + 1] for n in range(4)]
                over_sector = coupled(coupled(corner, factors[0], 0), factors[1], 1)
                over_slab = coupled(coupled(corner, factors[2], 1), factors[3], 0)
                terms[low, side] = [sign * (a + b) for a, b in zip(over_sector, over_slab)]
        return terms

    def finish(acoustic, added):
        terms = corner_terms(acoustic)
        copies = []
        for v in range(NV):
            if acoustic:
                for half in range(2):
                    lanes = slice(half * LINE, (half + 1) * LINE)
                    part = added[half][:, v * LINE : (v + 1) * LINE].reshape(C1, C2, LINE)
                    total[v, :, :, lanes] = base[v, :, :, lanes] + part
            else:
                total[v] = base[v]
            for (low, side), term in terms.items():
                j = side * (C2 - 1)
                total[v, low * (C1 - 1), j : j + 1, :] += term[v]
            copies.append(pltpu.make_async_copy(total.at[v], out.at[v], done.at[v]))
            copies[-1].start()
        for copy in copies:
            copy.wait()

    @pl.when(section == 0)
    def _():
        finish(False, None)

    @pl.when(section != 0)
    def _():
        kinds = weights[...]
        masks = []
        for a in range(slabs):
            kind = jnp.broadcast_to(kinds[:, a : a + 1], (CAP, LINE))
            masks.append(jnp.concatenate([kind] * NV, axis=0))
        placed = []
        for w in range(NW):
            parts = []
            for a in range(slabs):
                parts.append(jnp.where(masks[a] == w, 1.0, 0.0).astype(BF16) * received[a])
            placed.append(jnp.concatenate(parts, axis=0))
        placed = jnp.concatenate(placed, axis=1)
        stacked = jnp.concatenate([blocks[w] for w in range(NW)], axis=1)
        products = lax.dot_general(
            placed, stacked, (((1,), (1,)), ((), ())), preferred_element_type=F32
        )
        lines = []
        for v in range(NV):
            rows = []
            for a in range(slabs):
                start = (a * NV + v) * CAP
                rows.append(products[start : start + CAP])
            lines.append(jnp.concatenate(rows, axis=0))
        lines = jnp.concatenate(lines, axis=1)
        high = lines.astype(BF16)
        low = (lines - high.astype(F32)).astype(BF16)
        lines = jnp.concatenate([high, low], axis=0)
        wanted = jnp.concatenate([targets[...]] * 2, axis=1)
        added = []
        for half in range(2):
            here = 2 * rows_of((C1 * C2, lines.shape[0]), 0) + half
            chosen = jnp.where(here == wanted, 0.25, 0.0).astype(BF16)
            added.append(jnp.dot(chosen, lines, preferred_element_type=F32))
        finish(True, added)


def shards(fields, coefficients, old_source, weight_blocks, send_ids, target_ids, weight_ids):
    current = fields[0]
    factors = coefficients[0]
    peers = lax.axis_size("sec") * lax.axis_size("ax")
    message = jax.ShapeDtypeStruct((PLANES, C1, C3), BF16)
    field = jax.ShapeDtypeStruct((NV, C1, C2, C3), F32)
    cells = pltpu.VMEM((NV, C1, C2, C3), F32)

    low_slab, high_slab, low_sector, high_sector, kept, kept_factors, kept_source = pl.pallas_call(
        pack_halos,
        in_specs=[ANY] * 3,
        out_specs=[VMEM] * 7,
        out_shape=[message] * 4 + [cells, pltpu.VMEM((3, C1, C2, C3), F32), cells],
        scratch_shapes=[pltpu.SemaphoreType.DMA((2 * NV + 3,))],
        compiler_params=PARAMS,
        name="pack_halos",
    )(off_chip(current), off_chip(factors), off_chip(old_source))
    left = shift(high_sector, "az", 1, True)
    right = shift(low_sector, "az", -1, True)
    below = shift(high_slab, "ax", 1, False)
    above = shift(low_slab, "ax", -1, False)

    inner = pl.pallas_call(
        inner_step,
        in_specs=[VMEM] * 3,
        out_specs=VMEM,
        out_shape=field,
        compiler_params=PARAMS,
        name="inner_step",
    )(kept, kept_factors, kept_source)
    stepped, packed = pl.pallas_call(
        first_step,
        in_specs=[VMEM] * 8,
        out_specs=[VMEM] * 2,
        out_shape=[field, pltpu.HBM((peers, CAP * NV, LINE), BF16)],
        input_output_aliases={1: 0},
        scratch_shapes=[pltpu.VMEM((2, NV, C1, C3), F32)],
        compiler_params=PARAMS,
        name="first_step",
    )(send_ids[0, 0].T, inner, kept, kept_factors, left, right, below, above)
    received = lax.all_to_all(packed, ("sec", "ax"), split_axis=0, concat_axis=0, tiled=True)
    base, paths = pl.pallas_call(
        second_step,
        in_specs=[VMEM] * 7,
        out_specs=[VMEM] * 2,
        out_shape=[
            field,
            jax.ShapeDtypeStruct((2, 2, 8, C3), F32),
        ],
        scratch_shapes=[pltpu.VMEM((4, NV, C1, C3), F32)],
        compiler_params=PARAMS,
        name="second_step",
    )(stepped, off_chip(current), off_chip(factors), left, right, below, above)
    advanced = pl.pallas_call(
        add_source,
        in_specs=[VMEM] * 6,
        out_specs=ANY,
        out_shape=jax.ShapeDtypeStruct((NV, C1, C2, C3), F32),
        scratch_shapes=[cells, pltpu.SemaphoreType.DMA((NV,))],
        compiler_params=PARAMS,
        name="add_source",
    )(
        target_ids.reshape(1, -1),
        weight_ids[0, 0].T,
        received,
        weight_blocks[0, 0],
        base,
        paths,
    )
    return advanced[None]


def solution(mesh):
    return jax.shard_map(
        shards,
        mesh=mesh,
        in_specs=(
            P("sec", None, "ax", "az", None),
            P("sec", None, "ax", "az", None),
            P(None, "ax", "az", None),
            P("ax", "az", None, None, None),
            P("ax", "az", None, None),
            P("ax", "az", None, None),
            P("ax", "az", None, None),
        ),
        out_specs=P("sec", None, "ax", "az", None),
        check_vma=False,
    )
```

```python
import jax
import jax.numpy as jnp
from jax import lax
from jax.experimental import pallas as pl
from jax.experimental.pallas import tpu as pltpu
from jax.sharding import PartitionSpec as P

F32 = jnp.float32
BF16 = jnp.bfloat16
NV = 4
C1 = 16
C2 = 16
C3 = 256
LINE = 128
CAP = 8
NW = 8

NEAR = 0
FAR = 4
COEF = 8
SOURCE = 11
PLANES = 15

VMEM = pl.BlockSpec(memory_space=pltpu.VMEM)
ANY = pl.BlockSpec(memory_space=pl.ANY)
SMEM = pl.BlockSpec(memory_space=pltpu.SMEM)
PARAMS = pltpu.CompilerParams(vmem_limit_bytes=16 << 20)


def off_chip(x):
    return pltpu.with_memory_space_constraint(x, pltpu.HBM)


def swap(x, axis, first, periodic):
    count = lax.axis_size(axis)
    pairs = []
    for i in range(first, count if periodic else count - 1, 2):
        pairs += [(i, (i + 1) % count), ((i + 1) % count, i)]
    return lax.ppermute(x, axis, pairs)


def is_early(sector, sectors):
    return sector % (sectors // 2) == 0


def swap_slabs(x, first, early):
    sections, slabs, sectors = (lax.axis_size(axis) for axis in ("sec", "ax", "az"))
    pairs = []
    for section in range(sections):
        for slab in range(first, slabs - 1, 2):
            for sector in range(sectors):
                if is_early(sector, sectors) == early:
                    low = (section * slabs + slab) * sectors + sector
                    pairs += [(low, low + sectors), (low + sectors, low)]
    return lax.ppermute(x, ("sec", "ax", "az"), pairs)


def joined(early, late):
    return early.astype(F32) + late.astype(F32)


def upper_first(axis):
    return lax.axis_index(axis) % 2 == 0


def rows_of(shape, axis):
    return lax.broadcasted_iota(jnp.int32, shape, axis)


def next_row(x, end):
    return jnp.where(rows_of(x.shape, 0) == x.shape[0] - 1, end, pltpu.roll(x, x.shape[0] - 1, 0))


def previous_row(x, end):
    return jnp.where(rows_of(x.shape, 0) == 0, end, pltpu.roll(x, 1, 0))


def next_lane(x):
    return pltpu.roll(x, x.shape[1] - 1, 1)


def previous_lane(x):
    return pltpu.roll(x, 1, 1)


def eddy_plane(cells, upper, lower, ends, factors, across):
    along = 1 - across
    scaled = [0.25 * factors[k] for k in range(3)]
    carried = [0.125 * cells[k] for k in range(3)]
    up = [scaled[k] - carried[k] for k in range(3)]
    down = [scaled[k] + carried[k] for k in range(3)]
    lanes = rows_of(cells[0].shape, 1)
    up[2] = jnp.where(lanes == C3 - 1, 0.0, up[2])
    down[2] = jnp.where(lanes == 0, 0.0, down[2])
    own = 1.0 - 2.0 * (scaled[0] + scaled[1] + scaled[2])
    results = []
    for v in range(NV):
        cell = cells[v]
        low_end, high_end = ends[v]
        result = own * cell + up[across] * upper[v] + down[across] * lower[v]
        result += up[along] * next_row(cell, high_end) + down[along] * previous_row(cell, low_end)
        result += up[2] * next_lane(cell) + down[2] * previous_lane(cell)
        results.append(result)
    return results


def acoustic_plane(cells, upper, lower, ends, factors, across, source):
    along = 1 - across
    lanes = rows_of(cells[0].shape, 1)
    scaled = [0.125 * factors[k] for k in range(3)]
    change = [[None] * NV for _ in range(3)]
    for v in range(NV):
        cell = cells[v]
        low_end, high_end = ends[v]
        change[across][v] = upper[v] - lower[v]
        change[along][v] = next_row(cell, high_end) - previous_row(cell, low_end)
        change[2][v] = jnp.where(lanes == C3 - 1, 0.0, next_lane(cell)) - jnp.where(
            lanes == 0, 0.0, previous_lane(cell)
        )
    results = []
    for v in range(NV):
        if v == 0:
            coupling = change[0][1] + change[1][2] + change[2][3]
        else:
            coupling = change[v - 1][0]
        result = cells[v] - 0.125 * coupling
        for k in range(3):
            result -= scaled[k] * change[k][v]
        if source is not None:
            result += 0.25 * source[v]
        results.append(result)
    return results


def plane_step(acoustic, cells, upper, lower, ends, factors, across, source):
    if acoustic:
        return acoustic_plane(cells, upper, lower, ends, factors, across, source)
    return eddy_plane(cells, upper, lower, ends, factors, across)


def column(ref, component, j):
    return ref[component, :, j, :]


def pack_halos(q, c, s, *rest):
    *outs, cells, factors, source, done = rest
    sector_first, sector_second, slab_first, slab_second = outs
    sector_up = upper_first("az")
    slab_up = upper_first("ax")
    parts = []
    for v in range(NV):
        parts.append((q.at[v], cells.at[v]))
    for k in range(3):
        parts.append((c.at[k], factors.at[k]))
    for v in range(NV):
        parts.append((s.at[v], source.at[v]))
    copies = [pltpu.make_async_copy(*part, done.at[n]) for n, part in enumerate(parts)]
    for copy in copies:
        copy.start()

    def fill(ref, component, plane, depth):
        high = jnp.where(slab_up, C1 - 1 - depth, depth)
        slab_first[plane] = ref[component, high].astype(BF16)
        slab_second[plane] = ref[component, C1 - 1 - high].astype(BF16)
        low = column(ref, component, depth)
        high = column(ref, component, C2 - 1 - depth)
        sector_first[plane] = jnp.where(sector_up, high, low).astype(BF16)
        sector_second[plane] = jnp.where(sector_up, low, high).astype(BF16)

    for n, copy in enumerate(copies):
        copy.wait()
        if n < NV:
            fill(cells, n, NEAR + n, 0)
            fill(cells, n, FAR + n, 1)
        elif n < NV + 3:
            fill(factors, n - NV, COEF + n - NV, 0)
        else:
            fill(source, n - NV - 3, SOURCE + n - NV - 3, 0)


def fields_of(message, start, count=NV):
    return [message[start + v].astype(F32) for v in range(count)]


def step_rows(acoustic, q, c, s, below, above, ends_of, out):
    def row(i, upper, lower):
        cells = [q[v, i] for v in range(NV)]
        factors = [c[k, i] for k in range(3)]
        source = None if s is None else [s[v, i] for v in range(NV)]
        results = plane_step(acoustic, cells, upper, lower, ends_of(i), factors, 0, source)
        for v in range(NV):
            out[v, i] = results[v]

    row(0, [q[v, 1] for v in range(NV)], below)
    row(C1 - 1, above, [q[v, C1 - 2] for v in range(NV)])

    @pl.loop(1, C1 - 1)
    def _(i):
        row(i, [q[v, i + 1] for v in range(NV)], [q[v, i - 1] for v in range(NV)])


def no_ends(i):
    nothing = jnp.zeros((1, C3), F32)
    return [(nothing, nothing)] * NV


def inner_step(q, c, s, out):
    section = lax.axis_index("sec")
    nothing = [jnp.zeros((C2, C3), F32)] * NV

    @pl.when(section == 0)
    def _():
        step_rows(False, q, c, None, nothing, nothing, no_ends, out)

    @pl.when(section != 0)
    def _():
        step_rows(True, q, c, s, nothing, nothing, no_ends, out)


def coupled(values, factor, k):
    results = [factor * value for value in values]
    results[0] += 0.125 * values[k + 1]
    results[k + 1] += 0.125 * values[0]
    return results


def border_terms(acoustic, near, flow, factor, k, side):
    sign = 1.0 - 2.0 * side
    if acoustic:
        return [sign * term for term in coupled(near, 0.125 * factor, k)]
    weight = 0.25 * factor + (sign * 0.125) * flow
    return [weight * value for value in near]


def first_step(ids, inner, q, c, *rest):
    *messages, stepped, packed, sides, faces = rest
    section = lax.axis_index("sec")
    slab = lax.axis_index("ax")
    slabs = packed.shape[0] // 2
    sector_first, early_first, early_second, sector_second, late_first, late_second = messages
    sector_up = jnp.where(upper_first("az"), 1, 0)
    slab_up = jnp.where(upper_first("ax"), 1, 0)
    for v in range(NV):
        plane = NEAR + v
        sides[sector_up, v] = sector_first[plane].astype(F32)
        sides[1 - sector_up, v] = sector_second[plane].astype(F32)
        faces[slab_up, v] = joined(early_first[plane], late_first[plane])
        faces[1 - slab_up, v] = joined(early_second[plane], late_second[plane])

    def add_borders(acoustic):
        for side in range(2):
            i = side * (C1 - 1)
            near = [faces[side, v] for v in range(NV)]
            terms = border_terms(acoustic, near, q[0, i], c[0, i], 0, side)
            for v in range(NV):
                stepped[v, i] += terms[v]
        for i in range(C1):
            for side in range(2):
                j = side * (C2 - 1)
                near = [sides[side, v, i : i + 1, :] for v in range(NV)]
                flow = q[1, i, j : j + 1, :]
                factor = c[1, i, j : j + 1, :]
                terms = border_terms(acoustic, near, flow, factor, 1, side)
                for v in range(NV):
                    stepped[v, i, j : j + 1, :] += terms[v]

    @pl.when(section == 0)
    def _():
        add_borders(False)

        listed = ids[...]
        columns = [listed[:, r : r + 1] for r in range(slabs)]
        lanes = rows_of((CAP, C1 * C2), 1)
        chosen = [jnp.where(lanes == (column >> 1), 1.0, 0.0) for column in columns]
        chosen = jnp.concatenate(chosen, axis=0).astype(BF16)
        picked = []
        for v in range(NV):
            cells = stepped[v].astype(BF16).reshape(C1 * C2, C3)
            picked.append(jnp.dot(chosen, cells, preferred_element_type=F32))
        for r in range(slabs):
            odd = jnp.broadcast_to(columns[r] & 1, (CAP, LINE)) == 1
            rows = []
            for v in range(NV):
                both = picked[v][r * CAP : (r + 1) * CAP]
                rows.append(jnp.where(odd, both[:, LINE:], both[:, :LINE]))
            packed[slabs + r] = jnp.concatenate(rows, axis=0).astype(BF16)

    @pl.when(section != 0)
    def _():
        add_borders(True)

    def send_corners(peer, i):
        rows = []
        for v in range(NV):
            for side in range(2):
                row = sides[side, v, i : i + 1, :]
                rows += [row[:, :LINE], row[:, LINE:]]
        rows.append(jnp.zeros((CAP * NV - len(rows), LINE), F32))
        packed[section * slabs + peer] = jnp.concatenate(rows, axis=0).astype(BF16)

    @pl.when(slab > 0)
    def _():
        send_corners(slab - 1, 0)

    @pl.when(slab < slabs - 1)
    def _():
        send_corners(slab + 1, C1 - 1)


def ends_from(sides):
    def ends_of(i):
        return [(sides[0, v, pl.ds(i, 1), :], sides[1, v, pl.ds(i, 1), :]) for v in range(NV)]

    return ends_of


def second_step(stepped, q, c, *rest):
    *messages, out, paths, rims, halos = rest
    sector_first, early_first, early_second, sector_second, late_first, late_second = messages
    sector_up = jnp.where(upper_first("az"), 1, 0)
    slab_up = jnp.where(upper_first("ax"), 1, 0)
    halos[sector_up] = sector_first[...]
    halos[1 - sector_up] = sector_second[...]
    halos[2 + slab_up] = joined(early_first[...], late_first[...]).astype(BF16)
    halos[3 - slab_up] = joined(early_second[...], late_second[...]).astype(BF16)
    left, right, below, above = (halos.at[n] for n in range(4))
    section = lax.axis_index("sec")
    slab = lax.axis_index("ax")
    slabs = lax.axis_size("ax")

    def run(acoustic):
        nothing = jnp.zeros((1, C3), F32)
        ends = [(nothing, nothing)] * NV

        def rim(message, across, own, side):
            near = fields_of(message, NEAR)
            far = fields_of(message, FAR)
            upper, lower = (own, far) if side == 0 else (far, own)
            source = fields_of(message, SOURCE) if acoustic else None
            factors = fields_of(message, COEF, 3)
            return plane_step(acoustic, near, upper, lower, ends, factors, across, source)

        for side, message in enumerate((left, right)):
            own = [column(q, v, side * (C2 - 1)) for v in range(NV)]
            results = rim(message, 1, own, side)
            for v in range(NV):
                rims[side, v] = results[v]

        for side, message in enumerate((below, above)):
            own = [q[v, side * (C1 - 1)] for v in range(NV)]
            results = rim(message, 0, own, side)
            inside = slab > 0 if side == 0 else slab < slabs - 1
            for v in range(NV):
                rims[2 + side, v] = jnp.where(inside, results[v], 0.0)

        step_rows(
            acoustic,
            stepped,
            c,
            None,
            [rims[2, v] for v in range(NV)],
            [rims[3, v] for v in range(NV)],
            ends_from(rims),
            out,
        )

        for low in range(2):
            for side in range(2):
                i = low * (C1 - 1)
                j = side * (C2 - 1)
                slab_rim = (below, above)[low]
                sector_rim = (left, right)[side]

                def rim_row(message, plane, at):
                    return message[plane].astype(F32)[at : at + 1]

                if acoustic:
                    paths[low, side, 0:1] = 0.125 * rim_row(sector_rim, COEF, i)
                    paths[low, side, 1:2] = 0.125 * c[1, i, j : j + 1]
                    paths[low, side, 2:3] = 0.125 * rim_row(slab_rim, COEF + 1, j)
                    paths[low, side, 3:4] = 0.125 * c[0, i, j : j + 1]
                else:
                    toward_slab = 0.125 - 0.25 * low
                    toward_sector = 0.125 - 0.25 * side
                    over_sector = 0.25 * c[1, i, j : j + 1]
                    over_sector += toward_sector * stepped[1, i, j : j + 1]
                    over_sector *= 0.25 * rim_row(
                        sector_rim, COEF, i
                    ) + toward_slab * rim_row(sector_rim, NEAR, i)
                    over_slab = 0.25 * c[0, i, j : j + 1]
                    over_slab += toward_slab * stepped[0, i, j : j + 1]
                    over_slab *= 0.25 * rim_row(
                        slab_rim, COEF + 1, j
                    ) + toward_sector * rim_row(slab_rim, NEAR + 1, j)
                    paths[low, side, 0:1] = over_sector + over_slab

    @pl.when(section == 0)
    def _():
        run(False)

    @pl.when(section != 0)
    def _():
        run(True)


def add_source(targets, weights, received, blocks, base, paths, out, total, done):
    section = lax.axis_index("sec")
    slab = lax.axis_index("ax")
    slabs = received.shape[0] // 2

    def corner_terms(acoustic):
        terms = {}
        for low in range(2):
            inside = slab > 0 if low == 0 else slab < slabs - 1
            peer = jnp.clip(slab + 2 * low - 1, 0, slabs - 1)
            rows = received[section * slabs + peer].astype(F32)
            rows = jnp.where(inside, rows, 0.0)
            for side in range(2):
                corner = []
                for v in range(NV):
                    at = 2 * (2 * v + side)
                    corner.append(
                        jnp.concatenate([rows[at : at + 1], rows[at + 1 : at + 2]], axis=1)
                    )
                if not acoustic:
                    terms[low, side] = [paths[low, side, 0:1] * corner[v] for v in range(NV)]
                    continue
                sign = 1.0 if low == side else -1.0
                factors = [paths[low, side, n : n + 1] for n in range(4)]
                over_sector = coupled(coupled(corner, factors[0], 0), factors[1], 1)
                over_slab = coupled(coupled(corner, factors[2], 1), factors[3], 0)
                terms[low, side] = [sign * (a + b) for a, b in zip(over_sector, over_slab)]
        return terms

    def finish(acoustic, added):
        terms = corner_terms(acoustic)
        copies = []
        for v in range(NV):
            if acoustic:
                for half in range(2):
                    lanes = slice(half * LINE, (half + 1) * LINE)
                    part = added[half][:, v * LINE : (v + 1) * LINE].reshape(C1, C2, LINE)
                    total[v, :, :, lanes] = base[v, :, :, lanes] + part
            else:
                total[v] = base[v]
            for (low, side), term in terms.items():
                j = side * (C2 - 1)
                total[v, low * (C1 - 1), j : j + 1, :] += term[v]
            copies.append(pltpu.make_async_copy(total.at[v], out.at[v], done.at[v]))
            copies[-1].start()
        for copy in copies:
            copy.wait()

    @pl.when(section == 0)
    def _():
        finish(False, None)

    @pl.when(section != 0)
    def _():
        kinds = weights[...]
        masks = []
        for a in range(slabs):
            kind = jnp.broadcast_to(kinds[:, a : a + 1], (CAP, LINE))
            masks.append(jnp.concatenate([kind] * NV, axis=0))
        placed = []
        for w in range(NW):
            parts = []
            for a in range(slabs):
                parts.append(jnp.where(masks[a] == w, 1.0, 0.0).astype(BF16) * received[a])
            placed.append(jnp.concatenate(parts, axis=0))
        placed = jnp.concatenate(placed, axis=1)
        stacked = jnp.concatenate([blocks[w] for w in range(NW)], axis=1)
        products = lax.dot_general(
            placed, stacked, (((1,), (1,)), ((), ())), preferred_element_type=F32
        )
        lines = []
        for v in range(NV):
            rows = []
            for a in range(slabs):
                start = (a * NV + v) * CAP
                rows.append(products[start : start + CAP])
            lines.append(jnp.concatenate(rows, axis=0))
        lines = jnp.concatenate(lines, axis=1)
        high = lines.astype(BF16)
        low = (lines - high.astype(F32)).astype(BF16)
        lines = jnp.concatenate([high, low], axis=0)
        wanted = jnp.concatenate([targets[...]] * 2, axis=1)
        added = []
        for half in range(2):
            here = 2 * rows_of((C1 * C2, lines.shape[0]), 0) + half
            chosen = jnp.where(here == wanted, 0.25, 0.0).astype(BF16)
            added.append(jnp.dot(chosen, lines, preferred_element_type=F32))
        finish(True, added)


def shards(fields, coefficients, old_source, weight_blocks, send_ids, target_ids, weight_ids):
    current = fields[0]
    factors = coefficients[0]
    peers = lax.axis_size("sec") * lax.axis_size("ax")
    message = jax.ShapeDtypeStruct((PLANES, C1, C3), BF16)
    field = jax.ShapeDtypeStruct((NV, C1, C2, C3), F32)
    cells = pltpu.VMEM((NV, C1, C2, C3), F32)

    *sends, kept, kept_factors, kept_source = pl.pallas_call(
        pack_halos,
        in_specs=[ANY] * 3,
        out_specs=[VMEM] * 7,
        out_shape=[message] * 4 + [cells, pltpu.VMEM((3, C1, C2, C3), F32), cells],
        scratch_shapes=[pltpu.SemaphoreType.DMA((2 * NV + 3,))],
        compiler_params=PARAMS,
        name="pack_halos",
    )(off_chip(current), off_chip(factors), off_chip(old_source))
    sector_first = swap(sends[0], "az", 0, True)
    early = [swap_slabs(sends[2 + n], n, True) for n in range(2)]
    sector_second = swap(sends[1], "az", 1, True)
    sector_first, *sends = lax.optimization_barrier((sector_first, *sends))
    late = [swap_slabs(sends[2 + n], n, False) for n in range(2)]
    messages = [sector_first, early[0], early[1], sector_second, late[0], late[1]]
    inner = pl.pallas_call(
        inner_step,
        in_specs=[VMEM] * 3,
        out_specs=VMEM,
        out_shape=field,
        compiler_params=PARAMS,
        name="inner_step",
    )(kept, kept_factors, kept_source)
    stepped, packed = pl.pallas_call(
        first_step,
        in_specs=[VMEM] * 10,
        out_specs=[VMEM] * 2,
        out_shape=[field, pltpu.HBM((peers, CAP * NV, LINE), BF16)],
        input_output_aliases={1: 0},
        scratch_shapes=[pltpu.VMEM((2, NV, C1, C3), F32)] * 2,
        compiler_params=PARAMS,
        name="first_step",
    )(send_ids[0, 0].T, inner, kept, kept_factors, *messages)
    received = lax.all_to_all(packed, ("sec", "ax"), split_axis=0, concat_axis=0, tiled=True)
    base, paths = pl.pallas_call(
        second_step,
        in_specs=[VMEM] * 9,
        out_specs=[VMEM] * 2,
        out_shape=[
            field,
            jax.ShapeDtypeStruct((2, 2, 8, C3), F32),
        ],
        scratch_shapes=[
            pltpu.VMEM((4, NV, C1, C3), F32),
            pltpu.VMEM((4, PLANES, C1, C3), BF16),
        ],
        compiler_params=PARAMS,
        name="second_step",
    )(stepped, off_chip(current), off_chip(factors), *messages)
    advanced = pl.pallas_call(
        add_source,
        in_specs=[VMEM] * 6,
        out_specs=ANY,
        out_shape=jax.ShapeDtypeStruct((NV, C1, C2, C3), F32),
        scratch_shapes=[cells, pltpu.SemaphoreType.DMA((NV,))],
        compiler_params=PARAMS,
        name="add_source",
    )(
        target_ids.reshape(1, -1),
        weight_ids[0, 0].T,
        received,
        weight_blocks[0, 0],
        base,
        paths,
    )
    return advanced[None]


def solution(mesh):
    return jax.shard_map(
        shards,
        mesh=mesh,
        in_specs=(
            P("sec", None, "ax", "az", None),
            P("sec", None, "ax", "az", None),
            P(None, "ax", "az", None),
            P("ax", "az", None, None, None),
            P("ax", "az", None, None),
            P("ax", "az", None, None),
            P("ax", "az", None, None),
        ),
        out_specs=P("sec", None, "ax", "az", None),
        check_vma=False,
    )
```

```python
import jax
import jax.numpy as jnp
from jax import lax
from jax.experimental import pallas as pl
from jax.experimental.pallas import tpu as pltpu
from jax.sharding import PartitionSpec as P

F32 = jnp.float32
BF16 = jnp.bfloat16
NV = 4
C1 = 16
C2 = 16
C3 = 256
LINE = 128
CAP = 8
NW = 8

NEAR = 0
FAR = 4
COEF = 8
SOURCE = 11
PLANES = 15

VMEM = pl.BlockSpec(memory_space=pltpu.VMEM)
ANY = pl.BlockSpec(memory_space=pl.ANY)
SMEM = pl.BlockSpec(memory_space=pltpu.SMEM)
PARAMS = pltpu.CompilerParams(vmem_limit_bytes=16 << 20)


def off_chip(x):
    return pltpu.with_memory_space_constraint(x, pltpu.HBM)


def swap(x, axis, first, periodic):
    count = lax.axis_size(axis)
    pairs = []
    for i in range(first, count if periodic else count - 1, 2):
        pairs += [(i, (i + 1) % count), ((i + 1) % count, i)]
    return lax.ppermute(x, axis, pairs)


def is_early(sector, sectors):
    return sector % (sectors // 2) == 0


def swap_slabs(x, first, early):
    sections, slabs, sectors = (lax.axis_size(axis) for axis in ("sec", "ax", "az"))
    pairs = []
    for section in range(sections):
        for slab in range(first, slabs - 1, 2):
            for sector in range(sectors):
                if is_early(sector, sectors) == early:
                    low = (section * slabs + slab) * sectors + sector
                    pairs += [(low, low + sectors), (low + sectors, low)]
    return lax.ppermute(x, ("sec", "ax", "az"), pairs)


def joined(early, late):
    return early.astype(F32) + late.astype(F32)


def upper_first(axis):
    return lax.axis_index(axis) % 2 == 0


def rows_of(shape, axis):
    return lax.broadcasted_iota(jnp.int32, shape, axis)


def next_row(x, end):
    return jnp.where(rows_of(x.shape, 0) == x.shape[0] - 1, end, pltpu.roll(x, x.shape[0] - 1, 0))


def previous_row(x, end):
    return jnp.where(rows_of(x.shape, 0) == 0, end, pltpu.roll(x, 1, 0))


def next_lane(x):
    return pltpu.roll(x, x.shape[1] - 1, 1)


def previous_lane(x):
    return pltpu.roll(x, 1, 1)


def eddy_plane(cells, upper, lower, ends, factors, across):
    along = 1 - across
    scaled = [0.25 * factors[k] for k in range(3)]
    carried = [0.125 * cells[k] for k in range(3)]
    up = [scaled[k] - carried[k] for k in range(3)]
    down = [scaled[k] + carried[k] for k in range(3)]
    lanes = rows_of(cells[0].shape, 1)
    up[2] = jnp.where(lanes == C3 - 1, 0.0, up[2])
    down[2] = jnp.where(lanes == 0, 0.0, down[2])
    own = 1.0 - 2.0 * (scaled[0] + scaled[1] + scaled[2])
    results = []
    for v in range(NV):
        cell = cells[v]
        low_end, high_end = ends[v]
        result = own * cell + up[across] * upper[v] + down[across] * lower[v]
        result += up[along] * next_row(cell, high_end) + down[along] * previous_row(cell, low_end)
        result += up[2] * next_lane(cell) + down[2] * previous_lane(cell)
        results.append(result)
    return results


def acoustic_plane(cells, upper, lower, ends, factors, across, source):
    along = 1 - across
    lanes = rows_of(cells[0].shape, 1)
    scaled = [0.125 * factors[k] for k in range(3)]
    change = [[None] * NV for _ in range(3)]
    for v in range(NV):
        cell = cells[v]
        low_end, high_end = ends[v]
        change[across][v] = upper[v] - lower[v]
        change[along][v] = next_row(cell, high_end) - previous_row(cell, low_end)
        change[2][v] = jnp.where(lanes == C3 - 1, 0.0, next_lane(cell)) - jnp.where(
            lanes == 0, 0.0, previous_lane(cell)
        )
    results = []
    for v in range(NV):
        if v == 0:
            coupling = change[0][1] + change[1][2] + change[2][3]
        else:
            coupling = change[v - 1][0]
        result = cells[v] - 0.125 * coupling
        for k in range(3):
            result -= scaled[k] * change[k][v]
        if source is not None:
            result += 0.25 * source[v]
        results.append(result)
    return results


def plane_step(acoustic, cells, upper, lower, ends, factors, across, source):
    if acoustic:
        return acoustic_plane(cells, upper, lower, ends, factors, across, source)
    return eddy_plane(cells, upper, lower, ends, factors, across)


def column(ref, component, j):
    return ref[component, :, j, :]


def pack_halos(q, c, s, *rest):
    *outs, cells, factors, source, done = rest
    sector_first, sector_second, slab_first, slab_second = outs
    sector_up = upper_first("az")
    slab_up = upper_first("ax")
    parts = []
    for v in range(NV):
        parts.append((q.at[v], cells.at[v]))
    for k in range(3):
        parts.append((c.at[k], factors.at[k]))
    for v in range(NV):
        parts.append((s.at[v], source.at[v]))
    copies = [pltpu.make_async_copy(*part, done.at[n]) for n, part in enumerate(parts)]
    for copy in copies:
        copy.start()

    def fill(ref, component, plane, depth):
        high = jnp.where(slab_up, C1 - 1 - depth, depth)
        slab_first[plane] = ref[component, high].astype(BF16)
        slab_second[plane] = ref[component, C1 - 1 - high].astype(BF16)
        low = column(ref, component, depth)
        high = column(ref, component, C2 - 1 - depth)
        sector_first[plane] = jnp.where(sector_up, high, low).astype(BF16)
        sector_second[plane] = jnp.where(sector_up, low, high).astype(BF16)

    for n, copy in enumerate(copies):
        copy.wait()
        if n < NV:
            fill(cells, n, NEAR + n, 0)
            fill(cells, n, FAR + n, 1)
        elif n < NV + 3:
            fill(factors, n - NV, COEF + n - NV, 0)
        else:
            fill(source, n - NV - 3, SOURCE + n - NV - 3, 0)


def fields_of(message, start, count=NV):
    return [message[start + v].astype(F32) for v in range(count)]


def step_rows(acoustic, q, c, s, below, above, ends_of, out):
    def row(i, upper, lower):
        cells = [q[v, i] for v in range(NV)]
        factors = [c[k, i] for k in range(3)]
        source = None if s is None else [s[v, i] for v in range(NV)]
        results = plane_step(acoustic, cells, upper, lower, ends_of(i), factors, 0, source)
        for v in range(NV):
            out[v, i] = results[v]

    row(0, [q[v, 1] for v in range(NV)], below)
    row(C1 - 1, above, [q[v, C1 - 2] for v in range(NV)])

    @pl.loop(1, C1 - 1)
    def _(i):
        row(i, [q[v, i + 1] for v in range(NV)], [q[v, i - 1] for v in range(NV)])


def no_ends(i):
    nothing = jnp.zeros((1, C3), F32)
    return [(nothing, nothing)] * NV


def inner_step(q, c, s, out):
    section = lax.axis_index("sec")
    nothing = [jnp.zeros((C2, C3), F32)] * NV

    @pl.when(section == 0)
    def _():
        step_rows(False, q, c, None, nothing, nothing, no_ends, out)

    @pl.when(section != 0)
    def _():
        step_rows(True, q, c, s, nothing, nothing, no_ends, out)


def coupled(values, factor, k):
    results = [factor * value for value in values]
    results[0] += 0.125 * values[k + 1]
    results[k + 1] += 0.125 * values[0]
    return results


def border_terms(acoustic, near, flow, factor, k, side):
    sign = 1.0 - 2.0 * side
    if acoustic:
        return [sign * term for term in coupled(near, 0.125 * factor, k)]
    weight = 0.25 * factor + (sign * 0.125) * flow
    return [weight * value for value in near]


def first_step(ids, inner, q, c, *rest):
    *messages, stepped, packed, sides, faces = rest
    section = lax.axis_index("sec")
    slab = lax.axis_index("ax")
    slabs = packed.shape[0] // 2
    sector_first, early_second, early_first, sector_second, late_second, late_first = messages
    sector_up = jnp.where(upper_first("az"), 1, 0)
    slab_up = jnp.where(upper_first("ax"), 1, 0)
    for v in range(NV):
        plane = NEAR + v
        sides[sector_up, v] = sector_first[plane].astype(F32)
        sides[1 - sector_up, v] = sector_second[plane].astype(F32)
        faces[slab_up, v] = joined(early_first[plane], late_first[plane])
        faces[1 - slab_up, v] = joined(early_second[plane], late_second[plane])

    def add_borders(acoustic):
        for side in range(2):
            i = side * (C1 - 1)
            near = [faces[side, v] for v in range(NV)]
            terms = border_terms(acoustic, near, q[0, i], c[0, i], 0, side)
            for v in range(NV):
                stepped[v, i] += terms[v]
        for i in range(C1):
            for side in range(2):
                j = side * (C2 - 1)
                near = [sides[side, v, i : i + 1, :] for v in range(NV)]
                flow = q[1, i, j : j + 1, :]
                factor = c[1, i, j : j + 1, :]
                terms = border_terms(acoustic, near, flow, factor, 1, side)
                for v in range(NV):
                    stepped[v, i, j : j + 1, :] += terms[v]

    @pl.when(section == 0)
    def _():
        add_borders(False)

        listed = ids[...]
        columns = [listed[:, r : r + 1] for r in range(slabs)]
        lanes = rows_of((CAP, C1 * C2), 1)
        chosen = [jnp.where(lanes == (column >> 1), 1.0, 0.0) for column in columns]
        chosen = jnp.concatenate(chosen, axis=0).astype(BF16)
        picked = []
        for v in range(NV):
            cells = stepped[v].astype(BF16).reshape(C1 * C2, C3)
            picked.append(jnp.dot(chosen, cells, preferred_element_type=F32))
        for r in range(slabs):
            odd = jnp.broadcast_to(columns[r] & 1, (CAP, LINE)) == 1
            rows = []
            for v in range(NV):
                both = picked[v][r * CAP : (r + 1) * CAP]
                rows.append(jnp.where(odd, both[:, LINE:], both[:, :LINE]))
            packed[slabs + r] = jnp.concatenate(rows, axis=0).astype(BF16)

    @pl.when(section != 0)
    def _():
        add_borders(True)

    def send_corners(peer, i):
        rows = []
        for v in range(NV):
            for side in range(2):
                row = sides[side, v, i : i + 1, :]
                rows += [row[:, :LINE], row[:, LINE:]]
        rows.append(jnp.zeros((CAP * NV - len(rows), LINE), F32))
        packed[section * slabs + peer] = jnp.concatenate(rows, axis=0).astype(BF16)

    @pl.when(slab > 0)
    def _():
        send_corners(slab - 1, 0)

    @pl.when(slab < slabs - 1)
    def _():
        send_corners(slab + 1, C1 - 1)


def ends_from(sides):
    def ends_of(i):
        return [(sides[0, v, pl.ds(i, 1), :], sides[1, v, pl.ds(i, 1), :]) for v in range(NV)]

    return ends_of


def second_step(stepped, q, c, *rest):
    *messages, out, paths, rims, halos = rest
    sector_first, early_second, early_first, sector_second, late_second, late_first = messages
    sector_up = jnp.where(upper_first("az"), 1, 0)
    slab_up = jnp.where(upper_first("ax"), 1, 0)
    halos[sector_up] = sector_first[...]
    halos[1 - sector_up] = sector_second[...]
    halos[2 + slab_up] = joined(early_first[...], late_first[...]).astype(BF16)
    halos[3 - slab_up] = joined(early_second[...], late_second[...]).astype(BF16)
    left, right, below, above = (halos.at[n] for n in range(4))
    section = lax.axis_index("sec")
    slab = lax.axis_index("ax")
    slabs = lax.axis_size("ax")

    def run(acoustic):
        nothing = jnp.zeros((1, C3), F32)
        ends = [(nothing, nothing)] * NV

        def rim(message, across, own, side):
            near = fields_of(message, NEAR)
            far = fields_of(message, FAR)
            upper, lower = (own, far) if side == 0 else (far, own)
            source = fields_of(message, SOURCE) if acoustic else None
            factors = fields_of(message, COEF, 3)
            return plane_step(acoustic, near, upper, lower, ends, factors, across, source)

        for side, message in enumerate((left, right)):
            own = [column(q, v, side * (C2 - 1)) for v in range(NV)]
            results = rim(message, 1, own, side)
            for v in range(NV):
                rims[side, v] = results[v]

        for side, message in enumerate((below, above)):
            own = [q[v, side * (C1 - 1)] for v in range(NV)]
            results = rim(message, 0, own, side)
            inside = slab > 0 if side == 0 else slab < slabs - 1
            for v in range(NV):
                rims[2 + side, v] = jnp.where(inside, results[v], 0.0)

        step_rows(
            acoustic,
            stepped,
            c,
            None,
            [rims[2, v] for v in range(NV)],
            [rims[3, v] for v in range(NV)],
            ends_from(rims),
            out,
        )

        for low in range(2):
            for side in range(2):
                i = low * (C1 - 1)
                j = side * (C2 - 1)
                slab_rim = (below, above)[low]
                sector_rim = (left, right)[side]

                def rim_row(message, plane, at):
                    return message[plane].astype(F32)[at : at + 1]

                if acoustic:
                    paths[low, side, 0:1] = 0.125 * rim_row(sector_rim, COEF, i)
                    paths[low, side, 1:2] = 0.125 * c[1, i, j : j + 1]
                    paths[low, side, 2:3] = 0.125 * rim_row(slab_rim, COEF + 1, j)
                    paths[low, side, 3:4] = 0.125 * c[0, i, j : j + 1]
                else:
                    toward_slab = 0.125 - 0.25 * low
                    toward_sector = 0.125 - 0.25 * side
                    over_sector = 0.25 * c[1, i, j : j + 1]
                    over_sector += toward_sector * stepped[1, i, j : j + 1]
                    over_sector *= 0.25 * rim_row(
                        sector_rim, COEF, i
                    ) + toward_slab * rim_row(sector_rim, NEAR, i)
                    over_slab = 0.25 * c[0, i, j : j + 1]
                    over_slab += toward_slab * stepped[0, i, j : j + 1]
                    over_slab *= 0.25 * rim_row(
                        slab_rim, COEF + 1, j
                    ) + toward_sector * rim_row(slab_rim, NEAR + 1, j)
                    paths[low, side, 0:1] = over_sector + over_slab

    @pl.when(section == 0)
    def _():
        run(False)

    @pl.when(section != 0)
    def _():
        run(True)


def add_source(targets, weights, received, blocks, base, paths, out, total, done):
    section = lax.axis_index("sec")
    slab = lax.axis_index("ax")
    slabs = received.shape[0] // 2

    def corner_terms(acoustic):
        terms = {}
        for low in range(2):
            inside = slab > 0 if low == 0 else slab < slabs - 1
            peer = jnp.clip(slab + 2 * low - 1, 0, slabs - 1)
            rows = received[section * slabs + peer].astype(F32)
            rows = jnp.where(inside, rows, 0.0)
            for side in range(2):
                corner = []
                for v in range(NV):
                    at = 2 * (2 * v + side)
                    corner.append(
                        jnp.concatenate([rows[at : at + 1], rows[at + 1 : at + 2]], axis=1)
                    )
                if not acoustic:
                    terms[low, side] = [paths[low, side, 0:1] * corner[v] for v in range(NV)]
                    continue
                sign = 1.0 if low == side else -1.0
                factors = [paths[low, side, n : n + 1] for n in range(4)]
                over_sector = coupled(coupled(corner, factors[0], 0), factors[1], 1)
                over_slab = coupled(coupled(corner, factors[2], 1), factors[3], 0)
                terms[low, side] = [sign * (a + b) for a, b in zip(over_sector, over_slab)]
        return terms

    def finish(acoustic, added):
        terms = corner_terms(acoustic)
        copies = []
        for v in range(NV):
            if acoustic:
                for half in range(2):
                    lanes = slice(half * LINE, (half + 1) * LINE)
                    part = added[half][:, v * LINE : (v + 1) * LINE].reshape(C1, C2, LINE)
                    total[v, :, :, lanes] = base[v, :, :, lanes] + part
            else:
                total[v] = base[v]
            for (low, side), term in terms.items():
                j = side * (C2 - 1)
                total[v, low * (C1 - 1), j : j + 1, :] += term[v]
            copies.append(pltpu.make_async_copy(total.at[v], out.at[v], done.at[v]))
            copies[-1].start()
        for copy in copies:
            copy.wait()

    @pl.when(section == 0)
    def _():
        finish(False, None)

    @pl.when(section != 0)
    def _():
        kinds = weights[...]
        masks = []
        for a in range(slabs):
            kind = jnp.broadcast_to(kinds[:, a : a + 1], (CAP, LINE))
            masks.append(jnp.concatenate([kind] * NV, axis=0))
        placed = []
        for w in range(NW):
            parts = []
            for a in range(slabs):
                parts.append(jnp.where(masks[a] == w, 1.0, 0.0).astype(BF16) * received[a])
            placed.append(jnp.concatenate(parts, axis=0))
        placed = jnp.concatenate(placed, axis=1)
        stacked = jnp.concatenate([blocks[w] for w in range(NW)], axis=1)
        products = lax.dot_general(
            placed, stacked, (((1,), (1,)), ((), ())), preferred_element_type=F32
        )
        lines = []
        for v in range(NV):
            rows = []
            for a in range(slabs):
                start = (a * NV + v) * CAP
                rows.append(products[start : start + CAP])
            lines.append(jnp.concatenate(rows, axis=0))
        lines = jnp.concatenate(lines, axis=1)
        high = lines.astype(BF16)
        low = (lines - high.astype(F32)).astype(BF16)
        lines = jnp.concatenate([high, low], axis=0)
        wanted = jnp.concatenate([targets[...]] * 2, axis=1)
        added = []
        for half in range(2):
            here = 2 * rows_of((C1 * C2, lines.shape[0]), 0) + half
            chosen = jnp.where(here == wanted, 0.25, 0.0).astype(BF16)
            added.append(jnp.dot(chosen, lines, preferred_element_type=F32))
        finish(True, added)


def shards(fields, coefficients, old_source, weight_blocks, send_ids, target_ids, weight_ids):
    current = fields[0]
    factors = coefficients[0]
    peers = lax.axis_size("sec") * lax.axis_size("ax")
    message = jax.ShapeDtypeStruct((PLANES, C1, C3), BF16)
    field = jax.ShapeDtypeStruct((NV, C1, C2, C3), F32)
    cells = pltpu.VMEM((NV, C1, C2, C3), F32)

    *sends, kept, kept_factors, kept_source = pl.pallas_call(
        pack_halos,
        in_specs=[ANY] * 3,
        out_specs=[VMEM] * 7,
        out_shape=[message] * 4 + [cells, pltpu.VMEM((3, C1, C2, C3), F32), cells],
        scratch_shapes=[pltpu.SemaphoreType.DMA((2 * NV + 3,))],
        compiler_params=PARAMS,
        name="pack_halos",
    )(off_chip(current), off_chip(factors), off_chip(old_source))
    sector_first = swap(sends[0], "az", 0, True)
    early_second = swap_slabs(sends[3], 1, True)
    early_first = swap_slabs(sends[2], 0, True)
    sector_second = swap(sends[1], "az", 1, True)
    sector_first, *sends = lax.optimization_barrier((sector_first, *sends))
    late_second = swap_slabs(sends[3], 1, False)
    late_first = swap_slabs(sends[2], 0, False)
    messages = [sector_first, early_second, early_first, sector_second, late_second, late_first]
    inner = pl.pallas_call(
        inner_step,
        in_specs=[VMEM] * 3,
        out_specs=VMEM,
        out_shape=field,
        compiler_params=PARAMS,
        name="inner_step",
    )(kept, kept_factors, kept_source)
    stepped, packed = pl.pallas_call(
        first_step,
        in_specs=[VMEM] * 10,
        out_specs=[VMEM] * 2,
        out_shape=[field, pltpu.HBM((peers, CAP * NV, LINE), BF16)],
        input_output_aliases={1: 0},
        scratch_shapes=[pltpu.VMEM((2, NV, C1, C3), F32)] * 2,
        compiler_params=PARAMS,
        name="first_step",
    )(send_ids[0, 0].T, inner, kept, kept_factors, *messages)
    received = lax.all_to_all(packed, ("sec", "ax"), split_axis=0, concat_axis=0, tiled=True)
    base, paths = pl.pallas_call(
        second_step,
        in_specs=[VMEM] * 9,
        out_specs=[VMEM] * 2,
        out_shape=[
            field,
            jax.ShapeDtypeStruct((2, 2, 8, C3), F32),
        ],
        scratch_shapes=[
            pltpu.VMEM((4, NV, C1, C3), F32),
            pltpu.VMEM((4, PLANES, C1, C3), BF16),
        ],
        compiler_params=PARAMS,
        name="second_step",
    )(stepped, off_chip(current), off_chip(factors), *messages)
    advanced = pl.pallas_call(
        add_source,
        in_specs=[VMEM] * 6,
        out_specs=ANY,
        out_shape=jax.ShapeDtypeStruct((NV, C1, C2, C3), F32),
        scratch_shapes=[cells, pltpu.SemaphoreType.DMA((NV,))],
        compiler_params=PARAMS,
        name="add_source",
    )(
        target_ids.reshape(1, -1),
        weight_ids[0, 0].T,
        received,
        weight_blocks[0, 0],
        base,
        paths,
    )
    return advanced[None]


def solution(mesh):
    return jax.shard_map(
        shards,
        mesh=mesh,
        in_specs=(
            P("sec", None, "ax", "az", None),
            P("sec", None, "ax", "az", None),
            P(None, "ax", "az", None),
            P("ax", "az", None, None, None),
            P("ax", "az", None, None),
            P("ax", "az", None, None),
            P("ax", "az", None, None),
        ),
        out_specs=P("sec", None, "ax", "az", None),
        check_vma=False,
    )
```

```python
import functools

import jax
import jax.numpy as jnp
from jax import lax
from jax.experimental import pallas as pl
from jax.experimental.pallas import tpu as pltpu
from jax.sharding import PartitionSpec as P

F32 = jnp.float32
BF16 = jnp.bfloat16
NV = 4
C1 = 16
C2 = 16
C3 = 256
LINE = 128
CAP = 8
NW = 8

NEAR = 0
BEYOND = 4
COEF = 8
PLANES = 11

VMEM = pl.BlockSpec(memory_space=pltpu.VMEM)
ANY = pl.BlockSpec(memory_space=pl.ANY)
SMEM = pl.BlockSpec(memory_space=pltpu.SMEM)
PARAMS = pltpu.CompilerParams(vmem_limit_bytes=16 << 20)


def off_chip(x):
    return pltpu.with_memory_space_constraint(x, pltpu.HBM)


def shift_sectors(x, pairs):
    count = lax.axis_size("az")
    half = count // 2
    pairs = [
        ((source + start) % count, (target + start) % count)
        for start in (0, half)
        for source, target in pairs
    ]
    return lax.ppermute(x, "az", pairs)


def both_ways(firsts):
    return [pair for i in firsts for pair in ((i, i + 1), (i + 1, i))]


def is_early(sector, sectors):
    place = sector % (sectors // 2)
    return (place == 0) | (place == 1) | (place == 3)


def swap_slabs(x, first, early):
    sections, slabs, sectors = (lax.axis_size(axis) for axis in ("sec", "ax", "az"))
    pairs = []
    for section in range(sections):
        for slab in range(first, slabs - 1, 2):
            for sector in range(sectors):
                ahead = sector % (sectors // 2) == 0 if first == 0 else is_early(sector, sectors)
                if ahead == early:
                    low = (section * slabs + slab) * sectors + sector
                    pairs += [(low, low + sectors), (low + sectors, low)]
    return lax.ppermute(x, ("sec", "ax", "az"), pairs)


def joined(early, late):
    return early.astype(F32) + late.astype(F32)


def upper_first(axis):
    return lax.axis_index(axis) % 2 == 0


def rows_of(shape, axis):
    return lax.broadcasted_iota(jnp.int32, shape, axis)


def next_row(x, end):
    return jnp.where(rows_of(x.shape, 0) == x.shape[0] - 1, end, pltpu.roll(x, x.shape[0] - 1, 0))


def previous_row(x, end):
    return jnp.where(rows_of(x.shape, 0) == 0, end, pltpu.roll(x, 1, 0))


def next_lane(x):
    return pltpu.roll(x, x.shape[1] - 1, 1)


def previous_lane(x):
    return pltpu.roll(x, 1, 1)


def eddy_plane(cells, upper, lower, ends, factors, across):
    along = 1 - across
    scaled = [0.25 * factors[k] for k in range(3)]
    carried = [0.125 * cells[k] for k in range(3)]
    up = [scaled[k] - carried[k] for k in range(3)]
    down = [scaled[k] + carried[k] for k in range(3)]
    lanes = rows_of(cells[0].shape, 1)
    up[2] = jnp.where(lanes == C3 - 1, 0.0, up[2])
    down[2] = jnp.where(lanes == 0, 0.0, down[2])
    own = 1.0 - 2.0 * (scaled[0] + scaled[1] + scaled[2])
    results = []
    for v in range(NV):
        cell = cells[v]
        low_end, high_end = ends[v]
        result = own * cell + up[across] * upper[v] + down[across] * lower[v]
        result += up[along] * next_row(cell, high_end) + down[along] * previous_row(cell, low_end)
        result += up[2] * next_lane(cell) + down[2] * previous_lane(cell)
        results.append(result)
    return results


def acoustic_plane(cells, upper, lower, ends, factors, across, source):
    along = 1 - across
    lanes = rows_of(cells[0].shape, 1)
    scaled = [0.125 * factors[k] for k in range(3)]
    change = [[None] * NV for _ in range(3)]
    for v in range(NV):
        cell = cells[v]
        low_end, high_end = ends[v]
        change[across][v] = upper[v] - lower[v]
        change[along][v] = next_row(cell, high_end) - previous_row(cell, low_end)
        change[2][v] = jnp.where(lanes == C3 - 1, 0.0, next_lane(cell)) - jnp.where(
            lanes == 0, 0.0, previous_lane(cell)
        )
    results = []
    for v in range(NV):
        if v == 0:
            coupling = change[0][1] + change[1][2] + change[2][3]
        else:
            coupling = change[v - 1][0]
        result = cells[v] - 0.125 * coupling
        for k in range(3):
            result -= scaled[k] * change[k][v]
        if source is not None:
            result += 0.25 * source[v]
        results.append(result)
    return results


def plane_step(acoustic, cells, upper, lower, ends, factors, across, source):
    if acoustic:
        return acoustic_plane(cells, upper, lower, ends, factors, across, source)
    return eddy_plane(cells, upper, lower, ends, factors, across)


def column(ref, component, j):
    return ref[component, :, j, :]


def pack_halos(q, c, s, *rest):
    *outs, cells, factors, source, done = rest
    sector_first, sector_second, slab_first, slab_second = outs
    sector_up = upper_first("az")
    slab_up = upper_first("ax")
    parts = []
    for v in range(NV):
        parts.append((q.at[v], cells.at[v]))
    for k in range(3):
        parts.append((c.at[k], factors.at[k]))
    for v in range(NV):
        parts.append((s.at[v], source.at[v]))
    copies = [pltpu.make_async_copy(*part, done.at[n]) for n, part in enumerate(parts)]
    for copy in copies:
        copy.start()

    def slab(ref, component, depth, upper):
        return ref[component, jnp.where(upper, C1 - 1 - depth, depth)]

    def sector(ref, component, depth, upper):
        low = column(ref, component, depth)
        return jnp.where(upper, column(ref, component, C2 - 1 - depth), low)

    plans = []
    for first, second, take, up, k in (
        (sector_first, sector_second, sector, sector_up, 1),
        (slab_first, slab_second, slab, slab_up, 0),
    ):
        plans.append((first, take, up, k))
        plans.append((second, take, jnp.logical_not(up), k))

    for copy in copies[:NV]:
        copy.wait()
    near = []
    far = []
    for out, take, upper, k in plans:
        near.append([take(cells, v, 0, upper) for v in range(NV)])
        far.append([take(cells, v, 1, upper) for v in range(NV)])
        for v in range(NV):
            out[NEAR + v] = near[-1][v].astype(BF16)
    for copy in copies[NV : NV + 3]:
        copy.wait()
    factor = []
    for out, take, upper, k in plans:
        planes = [take(factors, n, 0, upper) for n in range(3)]
        factor.append(planes[k])
        for n in range(3):
            out[COEF + n] = planes[n].astype(BF16)
    for copy in copies[NV + 3 :]:
        copy.wait()

    def beyond(acoustic):
        for n, (out, take, upper, k) in enumerate(plans):
            sign = jnp.where(upper, 1.0, -1.0)
            terms = border_terms(acoustic, far[n], near[n][k], factor[n], k, sign)
            for v in range(NV):
                if acoustic:
                    terms[v] += 0.25 * take(source, v, 0, upper)
                out[BEYOND + v] = terms[v].astype(BF16)

    section = lax.axis_index("sec")

    @pl.when(section == 0)
    def _():
        beyond(False)

    @pl.when(section != 0)
    def _():
        beyond(True)


def fields_of(message, start, count=NV):
    return [message[start + v].astype(F32) for v in range(count)]


def step_rows(acoustic, q, c, s, below, above, ends_of, out):
    def row(i, upper, lower):
        cells = [q[v, i] for v in range(NV)]
        factors = [c[k, i] for k in range(3)]
        source = None if s is None else [s[v, i] for v in range(NV)]
        results = plane_step(acoustic, cells, upper, lower, ends_of(i), factors, 0, source)
        for v in range(NV):
            out[v, i] = results[v]

    row(0, [q[v, 1] for v in range(NV)], below)
    row(C1 - 1, above, [q[v, C1 - 2] for v in range(NV)])

    @pl.loop(1, C1 - 1)
    def _(i):
        row(i, [q[v, i + 1] for v in range(NV)], [q[v, i - 1] for v in range(NV)])


def no_ends(i):
    nothing = jnp.zeros((1, C3), F32)
    return [(nothing, nothing)] * NV


def inner_step(early, q, c, s, *rest):
    out = rest[-1]
    section = lax.axis_index("sec")
    mine = is_early(lax.axis_index("az"), lax.axis_size("az")) == early
    nothing = [jnp.zeros((C2, C3), F32)] * NV

    @pl.when(mine & (section == 0))
    def _():
        step_rows(False, q, c, None, nothing, nothing, no_ends, out)

    @pl.when(mine & (section != 0))
    def _():
        step_rows(True, q, c, s, nothing, nothing, no_ends, out)


def coupled(values, factor, k):
    results = [factor * value for value in values]
    results[0] += 0.125 * values[k + 1]
    results[k + 1] += 0.125 * values[0]
    return results


def border_terms(acoustic, near, flow, factor, k, sign):
    if acoustic:
        return [sign * term for term in coupled(near, 0.125 * factor, k)]
    weight = 0.25 * factor + (sign * 0.125) * flow
    return [weight * value for value in near]


def first_step(ids, inner, q, c, *rest):
    *messages, stepped, packed, sides, faces = rest
    section = lax.axis_index("sec")
    slab = lax.axis_index("ax")
    slabs = packed.shape[0] // 2
    wrapped, sector_first, early_second, early_first = messages[:4]
    sector_second, last_first, late_second, late_first = messages[4:]
    sector_up = jnp.where(upper_first("az"), 1, 0)
    slab_up = jnp.where(upper_first("ax"), 1, 0)
    for v in range(NV):
        plane = NEAR + v
        sides[sector_up, v] = joined(sector_first[plane], last_first[plane])
        sides[1 - sector_up, v] = joined(wrapped[plane], sector_second[plane])
        faces[slab_up, v] = joined(early_first[plane], late_first[plane])
        faces[1 - slab_up, v] = joined(early_second[plane], late_second[plane])

    def add_borders(acoustic):
        for side in range(2):
            i = side * (C1 - 1)
            near = [faces[side, v] for v in range(NV)]
            terms = border_terms(acoustic, near, q[0, i], c[0, i], 0, 1.0 - 2.0 * side)
            for v in range(NV):
                stepped[v, i] += terms[v]
        for i in range(C1):
            for side in range(2):
                j = side * (C2 - 1)
                near = [sides[side, v, i : i + 1, :] for v in range(NV)]
                flow = q[1, i, j : j + 1, :]
                factor = c[1, i, j : j + 1, :]
                terms = border_terms(acoustic, near, flow, factor, 1, 1.0 - 2.0 * side)
                for v in range(NV):
                    stepped[v, i, j : j + 1, :] += terms[v]

    @pl.when(section == 0)
    def _():
        add_borders(False)

        listed = ids[...]
        columns = [listed[:, r : r + 1] for r in range(slabs)]
        lanes = rows_of((CAP, C1 * C2), 1)
        chosen = [jnp.where(lanes == (column >> 1), 1.0, 0.0) for column in columns]
        chosen = jnp.concatenate(chosen, axis=0).astype(BF16)
        picked = []
        for v in range(NV):
            cells = stepped[v].astype(BF16).reshape(C1 * C2, C3)
            picked.append(jnp.dot(chosen, cells, preferred_element_type=F32))
        for r in range(slabs):
            odd = jnp.broadcast_to(columns[r] & 1, (CAP, LINE)) == 1
            rows = []
            for v in range(NV):
                both = picked[v][r * CAP : (r + 1) * CAP]
                rows.append(jnp.where(odd, both[:, LINE:], both[:, :LINE]))
            packed[slabs + r] = jnp.concatenate(rows, axis=0).astype(BF16)

    @pl.when(section != 0)
    def _():
        add_borders(True)

    def send_corners(peer, i):
        rows = []
        for v in range(NV):
            for side in range(2):
                row = sides[side, v, i : i + 1, :]
                rows += [row[:, :LINE], row[:, LINE:]]
        rows.append(jnp.zeros((CAP * NV - len(rows), LINE), F32))
        packed[section * slabs + peer] = jnp.concatenate(rows, axis=0).astype(BF16)

    @pl.when(slab > 0)
    def _():
        send_corners(slab - 1, 0)

    @pl.when(slab < slabs - 1)
    def _():
        send_corners(slab + 1, C1 - 1)


def ends_from(sides):
    def ends_of(i):
        return [(sides[0, v, pl.ds(i, 1), :], sides[1, v, pl.ds(i, 1), :]) for v in range(NV)]

    return ends_of


def second_step(stepped, q, c, *rest):
    *messages, out, paths, rims, halos = rest
    wrapped, sector_first, early_second, early_first = messages[:4]
    sector_second, last_first, late_second, late_first = messages[4:]
    sector_up = jnp.where(upper_first("az"), 1, 0)
    slab_up = jnp.where(upper_first("ax"), 1, 0)
    halos[sector_up] = joined(sector_first[...], last_first[...]).astype(BF16)
    halos[1 - sector_up] = joined(wrapped[...], sector_second[...]).astype(BF16)
    halos[2 + slab_up] = joined(early_first[...], late_first[...]).astype(BF16)
    halos[3 - slab_up] = joined(early_second[...], late_second[...]).astype(BF16)
    left, right, below, above = (halos.at[n] for n in range(4))
    section = lax.axis_index("sec")
    slab = lax.axis_index("ax")
    slabs = lax.axis_size("ax")

    def run(acoustic):
        nothing = jnp.zeros((1, C3), F32)
        ends = [(nothing, nothing)] * NV

        def rim(message, across, own, side):
            near = fields_of(message, NEAR)
            beyond = fields_of(message, BEYOND)
            none = [jnp.zeros((C1, C3), F32)] * NV
            upper, lower = (own, none) if side == 0 else (none, own)
            factors = fields_of(message, COEF, 3)
            results = plane_step(acoustic, near, upper, lower, ends, factors, across, None)
            return [results[v] + beyond[v] for v in range(NV)]

        for side, message in enumerate((left, right)):
            own = [column(q, v, side * (C2 - 1)) for v in range(NV)]
            results = rim(message, 1, own, side)
            for v in range(NV):
                rims[side, v] = results[v]

        for side, message in enumerate((below, above)):
            own = [q[v, side * (C1 - 1)] for v in range(NV)]
            results = rim(message, 0, own, side)
            inside = slab > 0 if side == 0 else slab < slabs - 1
            for v in range(NV):
                rims[2 + side, v] = jnp.where(inside, results[v], 0.0)

        step_rows(
            acoustic,
            stepped,
            c,
            None,
            [rims[2, v] for v in range(NV)],
            [rims[3, v] for v in range(NV)],
            ends_from(rims),
            out,
        )

        for low in range(2):
            for side in range(2):
                i = low * (C1 - 1)
                j = side * (C2 - 1)
                slab_rim = (below, above)[low]
                sector_rim = (left, right)[side]

                def rim_row(message, plane, at):
                    return message[plane].astype(F32)[at : at + 1]

                if acoustic:
                    paths[low, side, 0:1] = 0.125 * rim_row(sector_rim, COEF, i)
                    paths[low, side, 1:2] = 0.125 * c[1, i, j : j + 1]
                    paths[low, side, 2:3] = 0.125 * rim_row(slab_rim, COEF + 1, j)
                    paths[low, side, 3:4] = 0.125 * c[0, i, j : j + 1]
                else:
                    toward_slab = 0.125 - 0.25 * low
                    toward_sector = 0.125 - 0.25 * side
                    over_sector = 0.25 * c[1, i, j : j + 1]
                    over_sector += toward_sector * stepped[1, i, j : j + 1]
                    over_sector *= 0.25 * rim_row(
                        sector_rim, COEF, i
                    ) + toward_slab * rim_row(sector_rim, NEAR, i)
                    over_slab = 0.25 * c[0, i, j : j + 1]
                    over_slab += toward_slab * stepped[0, i, j : j + 1]
                    over_slab *= 0.25 * rim_row(
                        slab_rim, COEF + 1, j
                    ) + toward_sector * rim_row(slab_rim, NEAR + 1, j)
                    paths[low, side, 0:1] = over_sector + over_slab

    @pl.when(section == 0)
    def _():
        run(False)

    @pl.when(section != 0)
    def _():
        run(True)


def add_source(targets, weights, received, blocks, base, paths, out, total, done):
    section = lax.axis_index("sec")
    slab = lax.axis_index("ax")
    slabs = received.shape[0] // 2

    def corner_terms(acoustic):
        terms = {}
        for low in range(2):
            inside = slab > 0 if low == 0 else slab < slabs - 1
            peer = jnp.clip(slab + 2 * low - 1, 0, slabs - 1)
            rows = received[section * slabs + peer].astype(F32)
            rows = jnp.where(inside, rows, 0.0)
            for side in range(2):
                corner = []
                for v in range(NV):
                    at = 2 * (2 * v + side)
                    corner.append(
                        jnp.concatenate([rows[at : at + 1], rows[at + 1 : at + 2]], axis=1)
                    )
                if not acoustic:
                    terms[low, side] = [paths[low, side, 0:1] * corner[v] for v in range(NV)]
                    continue
                sign = 1.0 if low == side else -1.0
                factors = [paths[low, side, n : n + 1] for n in range(4)]
                over_sector = coupled(coupled(corner, factors[0], 0), factors[1], 1)
                over_slab = coupled(coupled(corner, factors[2], 1), factors[3], 0)
                terms[low, side] = [sign * (a + b) for a, b in zip(over_sector, over_slab)]
        return terms

    def finish(acoustic, added):
        terms = corner_terms(acoustic)
        copies = []
        for v in range(NV):
            if acoustic:
                for half in range(2):
                    lanes = slice(half * LINE, (half + 1) * LINE)
                    part = added[half][:, v * LINE : (v + 1) * LINE].reshape(C1, C2, LINE)
                    total[v, :, :, lanes] = base[v, :, :, lanes] + part
            else:
                total[v] = base[v]
            for (low, side), term in terms.items():
                j = side * (C2 - 1)
                total[v, low * (C1 - 1), j : j + 1, :] += term[v]
            copies.append(pltpu.make_async_copy(total.at[v], out.at[v], done.at[v]))
            copies[-1].start()
        for copy in copies:
            copy.wait()

    @pl.when(section == 0)
    def _():
        finish(False, None)

    @pl.when(section != 0)
    def _():
        kinds = weights[...]
        owners = [jnp.broadcast_to(kinds[:, a : a + 1], (CAP, LINE)) for a in range(slabs)]
        given = [received[a] for a in range(slabs)]
        placed = []
        for w in range(NW):
            parts = []
            for a in range(slabs):
                mask = jnp.where(owners[a] == w, 1.0, 0.0)
                mask = jnp.concatenate([mask, mask], axis=0).astype(BF16)
                for start in range(0, CAP * NV, 2 * CAP):
                    parts.append(mask * given[a][start : start + 2 * CAP])
            placed.append(jnp.concatenate(parts, axis=0))
        placed = jnp.concatenate(placed, axis=1)
        stacked = jnp.concatenate([blocks[w] for w in range(NW)], axis=1)
        products = lax.dot_general(
            placed, stacked, (((1,), (1,)), ((), ())), preferred_element_type=F32
        )
        lines = []
        for v in range(NV):
            rows = []
            for a in range(slabs):
                start = (a * NV + v) * CAP
                rows.append(products[start : start + CAP])
            lines.append(jnp.concatenate(rows, axis=0))
        lines = jnp.concatenate(lines, axis=1)
        high = lines.astype(BF16)
        low = (lines - high.astype(F32)).astype(BF16)
        lines = jnp.concatenate([high, low], axis=0)
        wanted = jnp.concatenate([targets[...]] * 2, axis=1)
        added = []
        for half in range(2):
            here = 2 * rows_of((C1 * C2, lines.shape[0]), 0) + half
            chosen = jnp.where(here == wanted, 0.25, 0.0).astype(BF16)
            added.append(jnp.dot(chosen, lines, preferred_element_type=F32))
        finish(True, added)


def shards(fields, coefficients, old_source, weight_blocks, send_ids, target_ids, weight_ids):
    current = fields[0]
    factors = coefficients[0]
    peers = lax.axis_size("sec") * lax.axis_size("ax")
    message = jax.ShapeDtypeStruct((PLANES, C1, C3), BF16)
    field = jax.ShapeDtypeStruct((NV, C1, C2, C3), F32)
    cells = pltpu.VMEM((NV, C1, C2, C3), F32)

    *sends, kept, kept_factors, kept_source = pl.pallas_call(
        pack_halos,
        in_specs=[ANY] * 3,
        out_specs=[VMEM] * 7,
        out_shape=[message] * 4 + [cells, pltpu.VMEM((3, C1, C2, C3), F32), cells],
        scratch_shapes=[pltpu.SemaphoreType.DMA((2 * NV + 3,))],
        compiler_params=PARAMS,
        name="pack_halos",
    )(off_chip(current), off_chip(factors), off_chip(old_source))
    last = lax.axis_size("az") // 2 - 1
    wrapped = shift_sectors(sends[1], [(last, last + 1)])
    sector_first = shift_sectors(sends[0], both_ways(range(0, last - 1, 2)))
    early_second = swap_slabs(sends[3], 1, True)
    early_first = swap_slabs(sends[2], 0, True)
    inner = pl.pallas_call(
        functools.partial(inner_step, True),
        in_specs=[VMEM] * 3,
        out_specs=VMEM,
        out_shape=field,
        compiler_params=PARAMS,
        name="inner_step_early",
    )(kept, kept_factors, kept_source)
    inner, sends[1] = lax.optimization_barrier((inner, sends[1]))
    sector_second = shift_sectors(sends[1], both_ways(range(1, last - 1, 2)) + [(last + 1, last)])
    sector_first, *sends = lax.optimization_barrier((sector_first, *sends))
    last_first = shift_sectors(sends[0], both_ways([last - 1]))
    late_second = swap_slabs(sends[3], 1, False)
    late_first = swap_slabs(sends[2], 0, False)
    messages = [wrapped, sector_first, early_second, early_first]
    messages += [sector_second, last_first, late_second, late_first]
    inner = pl.pallas_call(
        functools.partial(inner_step, False),
        in_specs=[VMEM] * 4,
        out_specs=VMEM,
        out_shape=field,
        input_output_aliases={3: 0},
        compiler_params=PARAMS,
        name="inner_step_late",
    )(kept, kept_factors, kept_source, inner)
    stepped, packed = pl.pallas_call(
        first_step,
        in_specs=[VMEM] * 12,
        out_specs=[VMEM] * 2,
        out_shape=[field, pltpu.HBM((peers, CAP * NV, LINE), BF16)],
        input_output_aliases={1: 0},
        scratch_shapes=[pltpu.VMEM((2, NV, C1, C3), F32)] * 2,
        compiler_params=PARAMS,
        name="first_step",
    )(send_ids[0, 0].T, inner, kept, kept_factors, *messages)
    received = lax.all_to_all(packed, ("sec", "ax"), split_axis=0, concat_axis=0, tiled=True)
    base, paths = pl.pallas_call(
        second_step,
        in_specs=[VMEM] * 11,
        out_specs=[VMEM] * 2,
        out_shape=[
            field,
            jax.ShapeDtypeStruct((2, 2, 8, C3), F32),
        ],
        scratch_shapes=[
            pltpu.VMEM((4, NV, C1, C3), F32),
            pltpu.VMEM((4, PLANES, C1, C3), BF16),
        ],
        compiler_params=PARAMS,
        name="second_step",
    )(stepped, off_chip(current), off_chip(factors), *messages)
    advanced = pl.pallas_call(
        add_source,
        in_specs=[VMEM] * 6,
        out_specs=ANY,
        out_shape=jax.ShapeDtypeStruct((NV, C1, C2, C3), F32),
        scratch_shapes=[cells, pltpu.SemaphoreType.DMA((NV,))],
        compiler_params=PARAMS,
        name="add_source",
    )(
        target_ids.reshape(1, -1),
        weight_ids[0, 0].T,
        received,
        weight_blocks[0, 0],
        base,
        paths,
    )
    return advanced[None]


def solution(mesh):
    return jax.shard_map(
        shards,
        mesh=mesh,
        in_specs=(
            P("sec", None, "ax", "az", None),
            P("sec", None, "ax", "az", None),
            P(None, "ax", "az", None),
            P("ax", "az", None, None, None),
            P("ax", "az", None, None),
            P("ax", "az", None, None),
            P("ax", "az", None, None),
        ),
        out_specs=P("sec", None, "ax", "az", None),
        check_vma=False,
    )
```

```python
import functools

import jax
import jax.numpy as jnp
from jax import lax
from jax.experimental import pallas as pl
from jax.experimental.pallas import tpu as pltpu
from jax.sharding import PartitionSpec as P

F32 = jnp.float32
BF16 = jnp.bfloat16
NV = 4
C1 = 16
C2 = 16
C3 = 256
LINE = 128
CAP = 8
NW = 8

NEAR = 0
BEYOND = 4
COEF = 8
PLANES = 11

VMEM = pl.BlockSpec(memory_space=pltpu.VMEM)
ANY = pl.BlockSpec(memory_space=pl.ANY)
SMEM = pl.BlockSpec(memory_space=pltpu.SMEM)
PARAMS = pltpu.CompilerParams(vmem_limit_bytes=16 << 20)


def off_chip(x):
    return pltpu.with_memory_space_constraint(x, pltpu.HBM)


def shift_sectors(x, pairs):
    count = lax.axis_size("az")
    half = count // 2
    pairs = [
        ((source + start) % count, (target + start) % count)
        for start in (0, half)
        for source, target in pairs
    ]
    return lax.ppermute(x, "az", pairs)


def both_ways(firsts):
    return [pair for i in firsts for pair in ((i, i + 1), (i + 1, i))]


def is_early(sector, sectors):
    place = sector % (sectors // 2)
    return (place == 0) | (place == 1) | (place == 3)


def swap_slabs(x, first, early):
    sections, slabs, sectors = (lax.axis_size(axis) for axis in ("sec", "ax", "az"))
    pairs = []
    for section in range(sections):
        for slab in range(first, slabs - 1, 2):
            for sector in range(sectors):
                ahead = sector % (sectors // 2) == 0 if first == 0 else is_early(sector, sectors)
                if ahead == early:
                    low = (section * slabs + slab) * sectors + sector
                    pairs += [(low, low + sectors), (low + sectors, low)]
    return lax.ppermute(x, ("sec", "ax", "az"), pairs)


def joined(early, late):
    return early.astype(F32) + late.astype(F32)


def upper_first(axis):
    return lax.axis_index(axis) % 2 == 0


def rows_of(shape, axis):
    return lax.broadcasted_iota(jnp.int32, shape, axis)


def next_row(x, end):
    return jnp.where(rows_of(x.shape, 0) == x.shape[0] - 1, end, pltpu.roll(x, x.shape[0] - 1, 0))


def previous_row(x, end):
    return jnp.where(rows_of(x.shape, 0) == 0, end, pltpu.roll(x, 1, 0))


def next_lane(x):
    return pltpu.roll(x, x.shape[1] - 1, 1)


def previous_lane(x):
    return pltpu.roll(x, 1, 1)


def eddy_plane(cells, upper, lower, ends, factors, across):
    along = 1 - across
    scaled = [0.25 * factors[k] for k in range(3)]
    carried = [0.125 * cells[k] for k in range(3)]
    up = [scaled[k] - carried[k] for k in range(3)]
    down = [scaled[k] + carried[k] for k in range(3)]
    lanes = rows_of(cells[0].shape, 1)
    up[2] = jnp.where(lanes == C3 - 1, 0.0, up[2])
    down[2] = jnp.where(lanes == 0, 0.0, down[2])
    own = 1.0 - 2.0 * (scaled[0] + scaled[1] + scaled[2])
    results = []
    for v in range(NV):
        cell = cells[v]
        low_end, high_end = ends[v]
        result = own * cell + up[across] * upper[v] + down[across] * lower[v]
        result += up[along] * next_row(cell, high_end) + down[along] * previous_row(cell, low_end)
        result += up[2] * next_lane(cell) + down[2] * previous_lane(cell)
        results.append(result)
    return results


def acoustic_plane(cells, upper, lower, ends, factors, across, source):
    along = 1 - across
    lanes = rows_of(cells[0].shape, 1)
    scaled = [0.125 * factors[k] for k in range(3)]
    change = [[None] * NV for _ in range(3)]
    for v in range(NV):
        cell = cells[v]
        low_end, high_end = ends[v]
        change[across][v] = upper[v] - lower[v]
        change[along][v] = next_row(cell, high_end) - previous_row(cell, low_end)
        change[2][v] = jnp.where(lanes == C3 - 1, 0.0, next_lane(cell)) - jnp.where(
            lanes == 0, 0.0, previous_lane(cell)
        )
    results = []
    for v in range(NV):
        if v == 0:
            coupling = change[0][1] + change[1][2] + change[2][3]
        else:
            coupling = change[v - 1][0]
        result = cells[v] - 0.125 * coupling
        for k in range(3):
            result -= scaled[k] * change[k][v]
        if source is not None:
            result += 0.25 * source[v]
        results.append(result)
    return results


def plane_step(acoustic, cells, upper, lower, ends, factors, across, source):
    if acoustic:
        return acoustic_plane(cells, upper, lower, ends, factors, across, source)
    return eddy_plane(cells, upper, lower, ends, factors, across)


def column(ref, component, j):
    return ref[component, :, j, :]


def pack_halos(q, c, s, ids, *rest):
    *outs, cells, factors, source, listed, done, held = rest
    sector_first, sector_second, slab_first, slab_second = outs
    sector_up = upper_first("az")
    slab_up = upper_first("ax")
    parts = []
    for v in range(NV):
        parts.append((q.at[v], cells.at[v]))
    for k in range(3):
        parts.append((c.at[k], factors.at[k]))
    for v in range(NV):
        parts.append((s.at[v], source.at[v]))
    parts.append((ids, listed))
    copies = [pltpu.make_async_copy(*part, done.at[n]) for n, part in enumerate(parts)]
    for copy in copies:
        copy.start()

    def slab(ref, component, depth, upper):
        return ref[component, jnp.where(upper, C1 - 1 - depth, depth)]

    def sector(ref, component, depth, upper):
        low = column(ref, component, depth)
        return jnp.where(upper, column(ref, component, C2 - 1 - depth), low)

    plans = []
    for first, second, take, up, k in (
        (sector_first, sector_second, sector, sector_up, 1),
        (slab_first, slab_second, slab, slab_up, 0),
    ):
        plans.append((first, take, up, k))
        plans.append((second, take, jnp.logical_not(up), k))

    for copy in copies[:NV]:
        copy.wait()
    near = []
    far = []
    for out, take, upper, k in plans:
        near.append([take(cells, v, 0, upper) for v in range(NV)])
        far.append([take(cells, v, 1, upper) for v in range(NV)])
        for v in range(NV):
            out[NEAR + v] = near[-1][v].astype(BF16)
    for copy in copies[NV : NV + 3]:
        copy.wait()
    factor = []
    for out, take, upper, k in plans:
        planes = [take(factors, n, 0, upper) for n in range(3)]
        factor.append(planes[k])
        for n in range(3):
            out[COEF + n] = planes[n].astype(BF16)
    def beyond(n, acoustic):
        upper, k = plans[n][2:]
        sign = jnp.where(upper, 1.0, -1.0)
        return border_terms(acoustic, far[n], near[n][k], factor[n], k, sign)

    section = lax.axis_index("sec")

    @pl.when(section == 0)
    def _():
        for n, plan in enumerate(plans):
            for v, term in enumerate(beyond(n, False)):
                plan[0][BEYOND + v] = term.astype(BF16)

    @pl.when(section != 0)
    def _():
        for n in range(len(plans)):
            for v, term in enumerate(beyond(n, True)):
                held[n, v] = term

    for copy in copies[NV + 3 :]:
        copy.wait()

    @pl.when(section != 0)
    def _():
        for n, (out, take, upper, k) in enumerate(plans):
            for v in range(NV):
                out[BEYOND + v] = (held[n, v] + 0.25 * take(source, v, 0, upper)).astype(BF16)


def fields_of(message, start, count=NV):
    return [message[start + v].astype(F32) for v in range(count)]


def step_rows(acoustic, q, c, s, below, above, ends_of, out):
    def row(i, upper, lower):
        cells = [q[v, i] for v in range(NV)]
        factors = [c[k, i] for k in range(3)]
        source = None if s is None else [s[v, i] for v in range(NV)]
        results = plane_step(acoustic, cells, upper, lower, ends_of(i), factors, 0, source)
        for v in range(NV):
            out[v, i] = results[v]

    row(0, [q[v, 1] for v in range(NV)], below)
    row(C1 - 1, above, [q[v, C1 - 2] for v in range(NV)])

    @pl.loop(1, C1 - 1)
    def _(i):
        row(i, [q[v, i + 1] for v in range(NV)], [q[v, i - 1] for v in range(NV)])


def no_ends(i):
    nothing = jnp.zeros((1, C3), F32)
    return [(nothing, nothing)] * NV


def inner_step(early, q, c, s, *rest):
    out = rest[-1]
    section = lax.axis_index("sec")
    mine = is_early(lax.axis_index("az"), lax.axis_size("az")) == early
    nothing = [jnp.zeros((C2, C3), F32)] * NV

    @pl.when(mine & (section == 0))
    def _():
        step_rows(False, q, c, None, nothing, nothing, no_ends, out)

    @pl.when(mine & (section != 0))
    def _():
        step_rows(True, q, c, s, nothing, nothing, no_ends, out)


def coupled(values, factor, k):
    results = [factor * value for value in values]
    results[0] += 0.125 * values[k + 1]
    results[k + 1] += 0.125 * values[0]
    return results


def border_terms(acoustic, near, flow, factor, k, sign):
    if acoustic:
        return [sign * term for term in coupled(near, 0.125 * factor, k)]
    weight = 0.25 * factor + (sign * 0.125) * flow
    return [weight * value for value in near]


def first_step(ids, inner, q, c, *rest):
    *messages, stepped, packed, sides, faces = rest
    section = lax.axis_index("sec")
    slab = lax.axis_index("ax")
    slabs = packed.shape[0] // 2
    wrapped, sector_first, early_second, early_first = messages[:4]
    sector_second, last_first, late_second, late_first = messages[4:]
    sector_up = jnp.where(upper_first("az"), 1, 0)
    slab_up = jnp.where(upper_first("ax"), 1, 0)
    for v in range(NV):
        plane = NEAR + v
        sides[sector_up, v] = joined(sector_first[plane], last_first[plane])
        sides[1 - sector_up, v] = joined(wrapped[plane], sector_second[plane])
        faces[slab_up, v] = joined(early_first[plane], late_first[plane])
        faces[1 - slab_up, v] = joined(early_second[plane], late_second[plane])

    def add_borders(acoustic):
        for side in range(2):
            i = side * (C1 - 1)
            near = [faces[side, v] for v in range(NV)]
            terms = border_terms(acoustic, near, q[0, i], c[0, i], 0, 1.0 - 2.0 * side)
            for v in range(NV):
                stepped[v, i] += terms[v]
        for i in range(C1):
            for side in range(2):
                j = side * (C2 - 1)
                near = [sides[side, v, i : i + 1, :] for v in range(NV)]
                flow = q[1, i, j : j + 1, :]
                factor = c[1, i, j : j + 1, :]
                terms = border_terms(acoustic, near, flow, factor, 1, 1.0 - 2.0 * side)
                for v in range(NV):
                    stepped[v, i, j : j + 1, :] += terms[v]

    @pl.when(section == 0)
    def _():
        add_borders(False)

        listed = ids[...]
        columns = [listed[:, r : r + 1] for r in range(slabs)]
        lanes = rows_of((CAP, C1 * C2), 1)
        chosen = [jnp.where(lanes == (column >> 1), 1.0, 0.0) for column in columns]
        chosen = jnp.concatenate(chosen, axis=0).astype(BF16)
        picked = []
        for v in range(NV):
            cells = stepped[v].astype(BF16).reshape(C1 * C2, C3)
            picked.append(jnp.dot(chosen, cells, preferred_element_type=F32))
        for r in range(slabs):
            odd = jnp.broadcast_to(columns[r] & 1, (CAP, LINE)) == 1
            rows = []
            for v in range(NV):
                both = picked[v][r * CAP : (r + 1) * CAP]
                rows.append(jnp.where(odd, both[:, LINE:], both[:, :LINE]))
            packed[slabs + r] = jnp.concatenate(rows, axis=0).astype(BF16)

    @pl.when(section != 0)
    def _():
        add_borders(True)

    def send_corners(peer, i):
        rows = []
        for v in range(NV):
            for side in range(2):
                row = sides[side, v, i : i + 1, :]
                rows += [row[:, :LINE], row[:, LINE:]]
        rows.append(jnp.zeros((CAP * NV - len(rows), LINE), F32))
        packed[section * slabs + peer] = jnp.concatenate(rows, axis=0).astype(BF16)

    @pl.when(slab > 0)
    def _():
        send_corners(slab - 1, 0)

    @pl.when(slab < slabs - 1)
    def _():
        send_corners(slab + 1, C1 - 1)


def ends_from(sides):
    def ends_of(i):
        return [(sides[0, v, pl.ds(i, 1), :], sides[1, v, pl.ds(i, 1), :]) for v in range(NV)]

    return ends_of


def second_step(stepped, q, c, *rest):
    *messages, out, paths, rims, halos = rest
    wrapped, sector_first, early_second, early_first = messages[:4]
    sector_second, last_first, late_second, late_first = messages[4:]
    sector_up = jnp.where(upper_first("az"), 1, 0)
    slab_up = jnp.where(upper_first("ax"), 1, 0)
    halos[sector_up] = joined(sector_first[...], last_first[...]).astype(BF16)
    halos[1 - sector_up] = joined(wrapped[...], sector_second[...]).astype(BF16)
    halos[2 + slab_up] = joined(early_first[...], late_first[...]).astype(BF16)
    halos[3 - slab_up] = joined(early_second[...], late_second[...]).astype(BF16)
    left, right, below, above = (halos.at[n] for n in range(4))
    section = lax.axis_index("sec")
    slab = lax.axis_index("ax")
    slabs = lax.axis_size("ax")

    def run(acoustic):
        nothing = jnp.zeros((1, C3), F32)
        ends = [(nothing, nothing)] * NV

        def rim(message, across, own, side):
            near = fields_of(message, NEAR)
            beyond = fields_of(message, BEYOND)
            none = [jnp.zeros((C1, C3), F32)] * NV
            upper, lower = (own, none) if side == 0 else (none, own)
            factors = fields_of(message, COEF, 3)
            results = plane_step(acoustic, near, upper, lower, ends, factors, across, None)
            return [results[v] + beyond[v] for v in range(NV)]

        for side, message in enumerate((left, right)):
            own = [column(q, v, side * (C2 - 1)) for v in range(NV)]
            results = rim(message, 1, own, side)
            for v in range(NV):
                rims[side, v] = results[v]

        for side, message in enumerate((below, above)):
            own = [q[v, side * (C1 - 1)] for v in range(NV)]
            results = rim(message, 0, own, side)
            inside = slab > 0 if side == 0 else slab < slabs - 1
            for v in range(NV):
                rims[2 + side, v] = jnp.where(inside, results[v], 0.0)

        step_rows(
            acoustic,
            stepped,
            c,
            None,
            [rims[2, v] for v in range(NV)],
            [rims[3, v] for v in range(NV)],
            ends_from(rims),
            out,
        )

        for low in range(2):
            for side in range(2):
                i = low * (C1 - 1)
                j = side * (C2 - 1)
                slab_rim = (below, above)[low]
                sector_rim = (left, right)[side]

                def rim_row(message, plane, at):
                    return message[plane].astype(F32)[at : at + 1]

                if acoustic:
                    paths[low, side, 0:1] = 0.125 * rim_row(sector_rim, COEF, i)
                    paths[low, side, 1:2] = 0.125 * c[1, i, j : j + 1]
                    paths[low, side, 2:3] = 0.125 * rim_row(slab_rim, COEF + 1, j)
                    paths[low, side, 3:4] = 0.125 * c[0, i, j : j + 1]
                else:
                    toward_slab = 0.125 - 0.25 * low
                    toward_sector = 0.125 - 0.25 * side
                    over_sector = 0.25 * c[1, i, j : j + 1]
                    over_sector += toward_sector * stepped[1, i, j : j + 1]
                    over_sector *= 0.25 * rim_row(
                        sector_rim, COEF, i
                    ) + toward_slab * rim_row(sector_rim, NEAR, i)
                    over_slab = 0.25 * c[0, i, j : j + 1]
                    over_slab += toward_slab * stepped[0, i, j : j + 1]
                    over_slab *= 0.25 * rim_row(
                        slab_rim, COEF + 1, j
                    ) + toward_sector * rim_row(slab_rim, NEAR + 1, j)
                    paths[low, side, 0:1] = over_sector + over_slab

    @pl.when(section == 0)
    def _():
        run(False)

    @pl.when(section != 0)
    def _():
        run(True)


def add_source(targets, weights, received, blocks, base, paths, out, total, done):
    section = lax.axis_index("sec")
    slab = lax.axis_index("ax")
    slabs = received.shape[0] // 2

    def corner_terms(acoustic):
        terms = {}
        for low in range(2):
            inside = slab > 0 if low == 0 else slab < slabs - 1
            peer = jnp.clip(slab + 2 * low - 1, 0, slabs - 1)
            rows = received[section * slabs + peer].astype(F32)
            rows = jnp.where(inside, rows, 0.0)
            for side in range(2):
                corner = []
                for v in range(NV):
                    at = 2 * (2 * v + side)
                    corner.append(
                        jnp.concatenate([rows[at : at + 1], rows[at + 1 : at + 2]], axis=1)
                    )
                if not acoustic:
                    terms[low, side] = [paths[low, side, 0:1] * corner[v] for v in range(NV)]
                    continue
                sign = 1.0 if low == side else -1.0
                factors = [paths[low, side, n : n + 1] for n in range(4)]
                over_sector = coupled(coupled(corner, factors[0], 0), factors[1], 1)
                over_slab = coupled(coupled(corner, factors[2], 1), factors[3], 0)
                terms[low, side] = [sign * (a + b) for a, b in zip(over_sector, over_slab)]
        return terms

    def finish(acoustic, added):
        terms = corner_terms(acoustic)
        copies = []
        for v in range(NV):
            if acoustic:
                for half in range(2):
                    lanes = slice(half * LINE, (half + 1) * LINE)
                    part = added[half][:, v * LINE : (v + 1) * LINE].reshape(C1, C2, LINE)
                    total[v, :, :, lanes] = base[v, :, :, lanes] + part
            else:
                total[v] = base[v]
            for (low, side), term in terms.items():
                j = side * (C2 - 1)
                total[v, low * (C1 - 1), j : j + 1, :] += term[v]
            copies.append(pltpu.make_async_copy(total.at[v], out.at[v], done.at[v]))
            copies[-1].start()
        for copy in copies:
            copy.wait()

    @pl.when(section == 0)
    def _():
        finish(False, None)

    @pl.when(section != 0)
    def _():
        kinds = weights[...]
        owners = [jnp.broadcast_to(kinds[:, a : a + 1], (CAP, LINE)) for a in range(slabs)]
        given = [received[a] for a in range(slabs)]
        placed = []
        for w in range(NW):
            parts = []
            for a in range(slabs):
                mask = jnp.where(owners[a] == w, 1.0, 0.0)
                mask = jnp.concatenate([mask, mask], axis=0).astype(BF16)
                for start in range(0, CAP * NV, 2 * CAP):
                    parts.append(mask * given[a][start : start + 2 * CAP])
            placed.append(jnp.concatenate(parts, axis=0))
        placed = jnp.concatenate(placed, axis=1)
        stacked = jnp.concatenate([blocks[w] for w in range(NW)], axis=1)
        products = lax.dot_general(
            placed, stacked, (((1,), (1,)), ((), ())), preferred_element_type=F32
        )
        lines = []
        for v in range(NV):
            rows = []
            for a in range(slabs):
                start = (a * NV + v) * CAP
                rows.append(products[start : start + CAP])
            lines.append(jnp.concatenate(rows, axis=0))
        lines = jnp.concatenate(lines, axis=1)
        high = lines.astype(BF16)
        low = (lines - high.astype(F32)).astype(BF16)
        lines = jnp.concatenate([high, low], axis=0)
        wanted = jnp.concatenate([targets[...]] * 2, axis=1)
        added = []
        for half in range(2):
            here = 2 * rows_of((C1 * C2, lines.shape[0]), 0) + half
            chosen = jnp.where(here == wanted, 0.25, 0.0).astype(BF16)
            added.append(jnp.dot(chosen, lines, preferred_element_type=F32))
        finish(True, added)


def shards(fields, coefficients, old_source, weight_blocks, send_ids, target_ids, weight_ids):
    current = fields[0]
    factors = coefficients[0]
    peers = lax.axis_size("sec") * lax.axis_size("ax")
    message = jax.ShapeDtypeStruct((PLANES, C1, C3), BF16)
    field = jax.ShapeDtypeStruct((NV, C1, C2, C3), F32)
    cells = pltpu.VMEM((NV, C1, C2, C3), F32)

    *sends, kept, kept_factors, kept_source, listed = pl.pallas_call(
        pack_halos,
        in_specs=[ANY] * 4,
        out_specs=[VMEM] * 8,
        out_shape=[message] * 4
        + [cells, pltpu.VMEM((3, C1, C2, C3), F32), cells]
        + [pltpu.VMEM((CAP, lax.axis_size("ax")), jnp.int32)],
        scratch_shapes=[
            pltpu.SemaphoreType.DMA((2 * NV + 4,)),
            pltpu.VMEM((4, NV, C1, C3), F32),
        ],
        compiler_params=PARAMS,
        name="pack_halos",
    )(
        off_chip(current),
        off_chip(factors),
        off_chip(old_source),
        off_chip(send_ids[0, 0].T),
    )
    last = lax.axis_size("az") // 2 - 1
    wrapped = shift_sectors(sends[1], [(last, last + 1)])
    sector_first = shift_sectors(sends[0], both_ways(range(0, last - 1, 2)))
    early_second = swap_slabs(sends[3], 1, True)
    early_first = swap_slabs(sends[2], 0, True)
    inner = pl.pallas_call(
        functools.partial(inner_step, True),
        in_specs=[VMEM] * 3,
        out_specs=VMEM,
        out_shape=field,
        compiler_params=PARAMS,
        name="inner_step_early",
    )(kept, kept_factors, kept_source)
    inner, sends[1] = lax.optimization_barrier((inner, sends[1]))
    sector_second = shift_sectors(sends[1], both_ways(range(1, last - 1, 2)) + [(last + 1, last)])
    sector_first, *sends = lax.optimization_barrier((sector_first, *sends))
    last_first = shift_sectors(sends[0], both_ways([last - 1]))
    late_second = swap_slabs(sends[3], 1, False)
    late_first = swap_slabs(sends[2], 0, False)
    messages = [wrapped, sector_first, early_second, early_first]
    messages += [sector_second, last_first, late_second, late_first]
    inner = pl.pallas_call(
        functools.partial(inner_step, False),
        in_specs=[VMEM] * 4,
        out_specs=VMEM,
        out_shape=field,
        input_output_aliases={3: 0},
        compiler_params=PARAMS,
        name="inner_step_late",
    )(kept, kept_factors, kept_source, inner)
    stepped, packed = pl.pallas_call(
        first_step,
        in_specs=[VMEM] * 12,
        out_specs=[VMEM] * 2,
        out_shape=[field, pltpu.HBM((peers, CAP * NV, LINE), BF16)],
        input_output_aliases={1: 0},
        scratch_shapes=[pltpu.VMEM((2, NV, C1, C3), F32)] * 2,
        compiler_params=PARAMS,
        name="first_step",
    )(listed, inner, kept, kept_factors, *messages)
    received = lax.all_to_all(packed, ("sec", "ax"), split_axis=0, concat_axis=0, tiled=True)
    base, paths = pl.pallas_call(
        second_step,
        in_specs=[VMEM] * 11,
        out_specs=[VMEM] * 2,
        out_shape=[
            field,
            jax.ShapeDtypeStruct((2, 2, 8, C3), F32),
        ],
        scratch_shapes=[
            pltpu.VMEM((4, NV, C1, C3), F32),
            pltpu.VMEM((4, PLANES, C1, C3), BF16),
        ],
        compiler_params=PARAMS,
        name="second_step",
    )(stepped, off_chip(current), off_chip(factors), *messages)
    advanced = pl.pallas_call(
        add_source,
        in_specs=[VMEM] * 6,
        out_specs=ANY,
        out_shape=jax.ShapeDtypeStruct((NV, C1, C2, C3), F32),
        scratch_shapes=[cells, pltpu.SemaphoreType.DMA((NV,))],
        compiler_params=PARAMS,
        name="add_source",
    )(
        target_ids.reshape(1, -1),
        weight_ids[0, 0].T,
        received,
        weight_blocks[0, 0],
        base,
        paths,
    )
    return advanced[None]


def solution(mesh):
    return jax.shard_map(
        shards,
        mesh=mesh,
        in_specs=(
            P("sec", None, "ax", "az", None),
            P("sec", None, "ax", "az", None),
            P(None, "ax", "az", None),
            P("ax", "az", None, None, None),
            P("ax", "az", None, None),
            P("ax", "az", None, None),
            P("ax", "az", None, None),
        ),
        out_specs=P("sec", None, "ax", "az", None),
        check_vma=False,
    )
```
